512 devices in a mesh: expert: 64 (over z, y), replica: 8 (over x, core).
Axes of the slice: x: 4, y: 4, z: 16, core: 2. Of those that a mesh axis runs over, the one named last changes fastest.
Arguments:
- grad_out: bfloat16 [16384, 2048], P(('expert', 'replica')), may hold values from -12 to 12
- routes: int32 [16384, 6], P(('expert', 'replica')), may hold values from 0 to 63, all different within a row; in each aligned block of 32 rows (0 to 31, 32 to 63, ...) at most 3 rows name the same one
- gates: float32 [16384, 6], P(('expert', 'replica')), may hold values from 0.03 to 0.6
- w_gate: bfloat16 [64, 1408, 2048], P('expert', 'replica'), may hold values from -0.125 to 0.125
- w_up: bfloat16 [64, 1408, 2048], P('expert', 'replica'), may hold values from -0.125 to 0.125
- w_down: bfloat16 [64, 1408, 2048], P('expert', 'replica'), may hold values from -0.15625 to 0.15625
- saved_gate: bfloat16 [64, 8, 64, 3, 1408], P('expert', 'replica'), may hold values from -8 to 8
- saved_up: bfloat16 [64, 8, 64, 3, 1408], P('expert', 'replica'), may hold values from -6 to 6
Outputs:
- grad_in: bfloat16 [16384, 2048], P(('expert', 'replica'))
The draws below stay inside these ranges and needn't reach their ends.
Inputs may be any that keep to these rules, and one draw needn't show every extreme that they name: `routes`: among the 32 tokens of one device, at most 3 entries name one expert; some expert is named 3 times; the 6 entries of a token differ.
All inputs are finite; a program needn't handle non-finite values.
Results may differ from the reference program's by a relative error of at most 0.01.
Values may be sent and summed in bfloat16 or wider, within the bound.
No kernel may reach another device: no remote copies, remote signals or barrier semaphores. Data moves between devices by JAX's collectives and lax.ppermute only.
A program may use at most 128 MiB of HBM per device.

```python
import math
import jax
import jax.numpy as jnp
import numpy as np
from jax import lax

D = 2048
HID = 1408
TOP = 6
TOK_DEV = 32
EXPERTS = 64
TOKENS = 16384
CAP = 3
N_EXPERT = 64
N_REPLICA = 8


def block_levels(rng, dims, split, low, top_value):
    factor_of = 1.0
    for dim, blocks in split:
        draws = jax.random.uniform(jax.random.fold_in(jax.random.fold_in(rng, 6), dim), (blocks,), jnp.float32, low / len(split), top_value / len(split))
        factor_of = factor_of * jnp.repeat(jnp.exp(draws), dims[dim] // blocks).reshape((-1,) + (1,) * (len(dims) - 1 - dim))
    return factor_of


def shared_out(key, own, number, rows, amount, top, bound, lean):
    sequence = jax.random.permutation(key, amount)
    crowded, common = portions_of(amount, rows * top, bound, lean, True), portions_of(amount, rows * top, bound, lean, False)
    places = jnp.arange(amount)

    def named(sizes, offset_by):
        used = int((sizes > 0).sum())
        fixed = max(1, used // 4)
        passed = fixed + (places - fixed + offset_by * (used - fixed)) % max(1, amount - fixed)
        return jnp.zeros((amount,), jnp.int32).at[sequence[jnp.where(places < fixed, places, passed)]].set(jnp.asarray(sizes, jnp.int32))

    sizes = jnp.where(number % 4 == 0, named(crowded, number // 4), named(common, number - number // 4 - 1))
    mixed = jax.random.permutation(jax.random.fold_in(own, 3), amount)
    giver, receiver = mixed[0:amount // 2 * 2:2], mixed[1:amount // 2 * 2:2]
    slack = jnp.minimum(sizes[giver] - 1, bound - sizes[receiver]) // 2
    slack = jnp.where((giver == sequence[0]) | (receiver == sequence[0]) | (sizes[receiver] == 0), 0, jnp.maximum(slack, 0))
    passed = jax.random.randint(jax.random.fold_in(own, 4), (amount // 2,), 0, 1 << 20) % (slack + 1)
    sizes = sizes.at[giver].add(-passed).at[receiver].add(passed)
    items = jnp.searchsorted(jnp.cumsum(sizes), jnp.arange(rows * top), side="right").astype(jnp.int32)
    table = items.reshape(top, rows).T
    table = table[jax.random.permutation(jax.random.fold_in(own, 1), rows)]
    offset_by = jax.random.randint(jax.random.fold_in(own, 2), (rows, 1), 0, top)
    return jnp.take_along_axis(table, (jnp.arange(top)[None, :] + offset_by) % top, axis=1)


def portions_of(number_of, total, reach, skew, full):
    weights = [(1 << 20) // math.isqrt(standing ** skew) + 1 for standing in range(1, number_of + 1)]
    largest = reach if full else min(reach, max(-(-total // number_of), total * weights[0] // sum(weights)))
    least = 1 if total - largest >= number_of - 1 else 0
    given, rest = [largest] + [least] * (number_of - 1), total - largest - least * (number_of - 1)
    while rest > 0:
        movable = [i for i in range(1, number_of) if given[i] < largest] or [i for i in range(1, number_of) if given[i] < reach]
        whole, budget = sum([weights[i] for i in movable]), rest
        for i in movable:
            extra = min(reach - given[i], max(1, budget * weights[i] // whole), rest)
            given[i] = given[i] + extra
            rest = rest - extra
    return np.array(given)


def scatter_about(stream_key, shape, deviation, most, split=(), kind=jnp.bfloat16):
    values = deviation * jax.random.normal(stream_key, shape, jnp.float32)
    if split:
        values = values * block_levels(stream_key, shape, split, -0.22, 0.18)
    return jnp.clip(values, -most, most).astype(kind)


def setup_inputs(seed: int = 0) -> dict:
    key_list = jax.random.split(jax.random.key(seed), 9)
    grad_out = scatter_about(key_list[0], (TOKENS, D), 2.0, 12.0, ((0, 512),))
    routes_keys = jax.random.split(jax.random.fold_in(key_list[1], 1), TOKENS // TOK_DEV)
    routes_turns = jax.random.permutation(jax.random.fold_in(key_list[1], 3), TOKENS // TOK_DEV)
    routes = jax.vmap(lambda own, number: shared_out(jax.random.fold_in(key_list[1], 2), own, number, TOK_DEV, EXPERTS, TOP, CAP, 2))(routes_keys, routes_turns).reshape((TOKENS, TOP))
    gates = jnp.clip(jnp.exp(math.log(0.6) - 2.9957323 * jax.random.uniform(key_list[2], (TOKENS, TOP), jnp.float32) ** block_levels(key_list[2], (TOKENS, TOP), ((0, 512),), -0.2, 0.2)), 0.03, 0.6)
    w_gate = scatter_about(key_list[3], (EXPERTS, HID, D), D ** -0.5, 0.125, ((0, 64), (1, 8)))
    w_up = scatter_about(key_list[4], (EXPERTS, HID, D), D ** -0.5, 0.125, ((0, 64), (1, 8)))
    w_down = scatter_about(key_list[5], (EXPERTS, HID, D), HID ** -0.5, 0.15625, ((0, 64), (1, 8)))
    saved_gate = scatter_about(key_list[6], (EXPERTS, N_REPLICA, N_EXPERT, CAP, HID), 1.5, 8.0, ((0, 64), (1, 8)))
    saved_up = scatter_about(key_list[7], (EXPERTS, N_REPLICA, N_EXPERT, CAP, HID), 1.0, 6.0, ((0, 64), (1, 8)))
    return {"grad_out": grad_out, "routes": routes, "gates": gates, "w_gate": w_gate, "w_up": w_up, "w_down": w_down, "saved_gate": saved_gate, "saved_up": saved_up}


def backward_rows(rows, saved_g, saved_u, gate_w, up_w, down_w):
    hidden_grad = lax.dot_general(rows, down_w, (((1,), (1,)), ((), ())), preferred_element_type=jnp.float32)
    gate_val = saved_g.astype(jnp.float32)
    up_val = saved_u.astype(jnp.float32)
    sigma = jax.nn.sigmoid(gate_val)
    up_grad = (hidden_grad * gate_val * sigma).astype(jnp.bfloat16)
    gate_grad = (hidden_grad * up_val * sigma * (1.0 + gate_val * (1.0 - sigma))).astype(jnp.bfloat16)
    return jnp.dot(gate_grad, gate_w, preferred_element_type=jnp.float32) + jnp.dot(up_grad, up_w, preferred_element_type=jnp.float32)


def reference(grad_out, routes, gates, w_gate, w_up, w_down, saved_gate, saved_up):
    blocks = N_EXPERT * N_REPLICA
    entries = TOK_DEV * TOP
    width_slice = HID // N_REPLICA
    flat = routes.reshape(blocks, entries).astype(jnp.int32)
    labels = jnp.arange(EXPERTS, dtype=jnp.int32)
    hot = (flat[:, :, None] == labels[None, None, :]).astype(jnp.int32)
    position = jnp.sum((jnp.cumsum(hot, axis=1) - hot) * hot, axis=2).astype(jnp.int32)
    block_id = jnp.arange(blocks, dtype=jnp.int32)[:, None] * jnp.ones((1, entries), jnp.int32)
    group = (block_id % N_REPLICA).astype(jnp.int32)
    source = (block_id // N_REPLICA).astype(jnp.int32)
    scaled = (gates[:, :, None] * grad_out[:, None, :].astype(jnp.float32)).astype(jnp.bfloat16)
    scaled = scaled.reshape(blocks, entries, D)
    buffer = jnp.zeros((EXPERTS, N_REPLICA, N_EXPERT, CAP, D), jnp.bfloat16)
    buffer = buffer.at[flat, group, source, position].set(scaled)

    def one_expert(items):
        rows, gate_w, up_w, down_w, saved_g, saved_u = items
        rows = rows.reshape(-1, D)
        saved_g = saved_g.reshape(-1, HID)
        saved_u = saved_u.reshape(-1, HID)
        total = jnp.zeros((rows.shape[0], D), jnp.float32)
        for index in range(N_REPLICA):
            low = index * width_slice
            high = low + width_slice
            term = backward_rows(rows, saved_g[:, low:high], saved_u[:, low:high], gate_w[low:high], up_w[low:high], down_w[low:high])
            rounded = lax.optimization_barrier(term.astype(jnp.bfloat16))
            total = total + rounded.astype(jnp.float32)
        return total.astype(jnp.bfloat16)

    results = lax.map(one_expert, (buffer, w_gate, w_up, w_down, saved_gate, saved_up))
    results = results.reshape(EXPERTS, N_REPLICA, N_EXPERT, CAP, D)
    picked = results[flat, group, source, position]
    summed = jnp.sum(picked.astype(jnp.float32).reshape(TOKENS, TOP, D), axis=1)
    return summed.astype(jnp.bfloat16)
```

```python
import functools
import jax
import jax.numpy as jnp
from jax import lax
from jax.experimental import pallas as pl
from jax.experimental.pallas import tpu as pltpu
from jax.sharding import PartitionSpec as P

F32 = jnp.float32
BF16 = jnp.bfloat16
VM = pl.BlockSpec(memory_space=pltpu.VMEM)
SM = pl.BlockSpec(memory_space=pltpu.SMEM)
LINKS = 4


def call(kernel, ins, outs, flops=0, smem=0):
    moved = sum(a.size * a.dtype.itemsize for a in ins) + sum(o.size * o.dtype.itemsize for o in outs)
    single = len(outs) == 1
    return pl.pallas_call(
        kernel,
        out_shape=outs[0] if single else tuple(outs),
        in_specs=[SM] * smem + [VM] * (len(ins) - smem),
        out_specs=VM if single else tuple([VM] * len(outs)),
        cost_estimate=pl.CostEstimate(flops=flops, bytes_accessed=moved, transcendentals=0),
    )(*ins)


def place_kernel(routes_ref, gates_ref, grad_ref, out_ref, hot_ref):
    top, tokens = routes_ref.shape
    rows = out_ref.shape[0]
    slots = 3
    row = lax.broadcasted_iota(jnp.int32, (rows, tokens), 0)
    named = row // slots
    slot = (row - named * slots).astype(F32)
    hits = jnp.zeros((rows, tokens), F32)
    gate = jnp.zeros((rows, tokens), F32)
    for k in range(top):
        hit = routes_ref[k : k + 1, :] == named
        hits = jnp.where(hit, 1.0, hits)
        gate = jnp.where(hit, gates_ref[k : k + 1, :], gate)
    before = (
        lax.broadcasted_iota(jnp.int32, (tokens, tokens), 0)
        < lax.broadcasted_iota(jnp.int32, (tokens, tokens), 1)
    ).astype(BF16)
    earlier = jnp.dot(hits.astype(BF16), before, preferred_element_type=F32)
    chosen = (hits > 0.5) & (jnp.abs(earlier - slot) < 0.5)
    weight = jnp.sum(jnp.where(chosen, gate, 0.0), axis=1, keepdims=True)
    hot = jnp.where(chosen, 1.0, 0.0).astype(BF16)
    hot_ref[...] = hot
    out_ref[...] = (weight * jnp.dot(hot, grad_ref[...], preferred_element_type=F32)).astype(BF16)


def select_kernel(index_ref, gate_ref, up_ref, keep_ref, send_ref):
    slice_width = keep_ref.shape[3]
    for j in range(2 * LINKS):
        place = index_ref[j]
        low = j * slice_width
        parts = (gate_ref[:, low : low + slice_width], up_ref[:, low : low + slice_width])

        @pl.when(index_ref[2 * LINKS + j] == 1)
        def _():
            keep_ref[0, place] = parts[0]
            keep_ref[1, place] = parts[1]

        @pl.when(index_ref[2 * LINKS + j] == 0)
        def _():
            send_ref[0, place] = parts[0]
            send_ref[1, place] = parts[1]


def factor_kernel(saved_ref, gate_ref, up_ref):
    for p in range(LINKS):
        g = saved_ref[0, p].astype(F32)
        u = saved_ref[1, p].astype(F32)
        sig = jax.nn.sigmoid(g)
        up_ref[p] = g * sig
        gate_ref[p] = u * sig * (1.0 + g * (1.0 - sig))


def hidden_kernel(rows_ref, own_ref, left_ref, right_ref, far1_ref, far2_ref, gf_ref, uf_ref, gate_ref, up_ref):
    def nt(a, b):
        return lax.dot_general(a, b, (((1,), (1,)), ((), ())), preferred_element_type=F32)

    half = far1_ref.shape[1]
    for p in range(LINKS):
        if p < 3:
            grad = nt(rows_ref[...], (own_ref, left_ref, right_ref)[p][...])
        else:
            grad = nt(rows_ref[:, :half], far1_ref[...]) + nt(rows_ref[:, half:], far2_ref[...])
        gate_ref[p] = (grad * gf_ref[p]).astype(BF16)
        up_ref[p] = (grad * uf_ref[p]).astype(BF16)


def output_kernel(gate_ref, up_ref, own_ref, left_ref, right_ref, farg_ref, faru_ref, *rest):
    out_ref = rest[-1]
    width = farg_ref.shape[0]

    def mm(a, b):
        return jnp.dot(a, b, preferred_element_type=F32)

    total = mm(gate_ref[3], farg_ref[...]) + mm(up_ref[3], faru_ref[...])
    for p, ref in enumerate((own_ref, left_ref, right_ref)):
        total += mm(gate_ref[p], ref[:width]) + mm(up_ref[p], ref[width:])
    if len(rest) == 2:
        total += rest[0][...].astype(F32)
    out_ref[...] = total.astype(out_ref.dtype)


def combine_kernel(hot_ref, *refs):
    out_ref = refs[-1]
    width = refs[0].shape[1]
    for n, ref in enumerate(refs[:-1]):
        total = lax.dot_general(hot_ref[...], ref[...], (((0,), (0,)), ((), ())), preferred_element_type=F32)
        out_ref[:, n * width : (n + 1) * width] = total.astype(BF16)


def body(grad_out, routes, gates, w_gate, w_up, w_down, saved_gate, saved_up):
    experts = lax.axis_size("expert")
    copies = lax.axis_size("replica")
    tokens, width = grad_out.shape
    slots = saved_gate.shape[3]
    slice_width = w_gate.shape[1]
    rows = experts * slots
    half = width // 2
    chunks = half // 128
    replica = lax.axis_index("replica")
    link, core = replica // 2, replica % 2

    def along(a, by):
        pairs = [(2 * i + k, 2 * ((i + by) % LINKS) + k) for i in range(LINKS) for k in range(2)]
        return lax.ppermute(a, "replica", pairs)

    def across(a):
        return lax.ppermute(a, "replica", [(i, i ^ 1) for i in range(copies)])

    down = w_down[0]
    down_left, down_right = along(down, 1), along(down, -1)

    placed, hot = call(
        place_kernel,
        (routes.T, gates.T, grad_out),
        (jax.ShapeDtypeStruct((rows, width), BF16), jax.ShapeDtypeStruct((rows, tokens), BF16)),
        2 * rows * tokens * width,
    )
    packed = placed.reshape(experts, slots * 2 * chunks, 128)
    arrived = lax.all_to_all(packed, "expert", split_axis=0, concat_axis=0, tiled=True)

    first = jnp.concatenate([w_gate[0, :, :half], w_up[0, :, :half]], axis=0)
    second = jnp.concatenate([w_gate[0, :, half:], w_up[0, :, half:]], axis=0)
    first_left, first_right = along(first, 1), along(first, -1)
    down_far1, down_far2 = along(down_left[:, :half], 1), along(down_right[:, half:], -1)
    second_left, second_right = along(second, 1), along(second, -1)
    first_farg, first_faru = along(first_left[:slice_width], 1), along(first_right[slice_width:], -1)
    second_farg, second_faru = along(second_left[:slice_width], 1), along(second_right[slice_width:], -1)

    order = jnp.arange(2 * LINKS, dtype=jnp.int32)
    offset = (order // 2 - link) % LINKS
    where = jnp.asarray([0, 2, 3, 1], jnp.int32)[offset]
    mine = (order % 2 == core).astype(jnp.int32)
    saved = tuple(a[0, 0].transpose(1, 0, 2).reshape(rows, -1) for a in (saved_gate, saved_up))
    piece = jax.ShapeDtypeStruct((2, LINKS, rows, slice_width), BF16)
    keep, send = call(select_kernel, (jnp.concatenate([where, mine]),) + saved, (piece, piece), smem=1)
    factor = jax.ShapeDtypeStruct((LINKS, rows, slice_width), F32)
    own_factors = call(factor_kernel, (keep,), (factor, factor))
    other_factors = call(factor_kernel, (across(send),), (factor, factor))

    own_rows = arrived.reshape(experts, slots, width).transpose(1, 0, 2).reshape(rows, width)
    other_rows = across(own_rows)
    downs = (down, down_left, down_right, down_far1, down_far2)
    hidden = jax.ShapeDtypeStruct((LINKS, rows, slice_width), BF16)
    cost = 2 * rows * LINKS * slice_width * width
    own_hidden = call(hidden_kernel, (own_rows,) + downs + tuple(own_factors), (hidden, hidden), cost)
    other_hidden = call(hidden_kernel, (other_rows,) + downs + tuple(other_factors), (hidden, hidden), cost)

    results = []
    for pieces in (
        (first, first_left, first_right, first_farg, first_faru),
        (second, second_left, second_right, second_farg, second_faru),
    ):
        part = jax.ShapeDtypeStruct((rows, half), BF16)
        theirs = call(output_kernel, tuple(other_hidden) + pieces, (part,), cost)
        total = call(output_kernel, tuple(own_hidden) + pieces + (across(theirs),), (part,), cost)
        outgoing = total.reshape(slots, experts, half).transpose(1, 0, 2).reshape(experts, slots * chunks, 128)
        back = lax.all_to_all(outgoing, "expert", split_axis=0, concat_axis=0, tiled=True)
        results.append(back.reshape(rows, half))
    return call(
        combine_kernel, (hot,) + tuple(results), (jax.ShapeDtypeStruct((tokens, width), BF16),)
    )


def solution(mesh):
    in_specs = (
        P(("expert", "replica"), None),
        P(("expert", "replica"), None),
        P(("expert", "replica"), None),
        P("expert", "replica", None),
        P("expert", "replica", None),
        P("expert", "replica", None),
        P("expert", "replica", None, None, None),
        P("expert", "replica", None, None, None),
    )
    out_specs = P(("expert", "replica"), None)
    return jax.shard_map(body, mesh=mesh, in_specs=in_specs, out_specs=out_specs, check_vma=False)
```

```python
import jax
import jax.numpy as jnp
from jax import lax
from jax.experimental import pallas as pl
from jax.experimental.pallas import tpu as pltpu
from jax.sharding import PartitionSpec as P

F32 = jnp.float32
BF16 = jnp.bfloat16
VM = pl.BlockSpec(memory_space=pltpu.VMEM)
SM = pl.BlockSpec(memory_space=pltpu.SMEM)
LINKS = 4


def call(kernel, ins, outs, flops=0, smem=0, scratch=()):
    moved = sum(a.size * a.dtype.itemsize for a in ins) + sum(o.size * o.dtype.itemsize for o in outs)
    single = len(outs) == 1
    return pl.pallas_call(
        kernel,
        out_shape=outs[0] if single else tuple(outs),
        in_specs=[SM] * smem + [VM] * (len(ins) - smem),
        out_specs=VM if single else tuple([VM] * len(outs)),
        scratch_shapes=list(scratch),
        cost_estimate=pl.CostEstimate(flops=flops, bytes_accessed=moved, transcendentals=0),
    )(*ins)


def pack(value, out_ref):
    experts, deep, lanes = out_ref.shape
    slots = value.shape[0] // experts
    chunks = deep // slots
    for s in range(slots):
        block = value[s * experts : (s + 1) * experts].astype(BF16)
        parts = jnp.stack([block[:, c * lanes : (c + 1) * lanes] for c in range(chunks)])
        out_ref[:, s * chunks : (s + 1) * chunks, :] = jnp.swapaxes(parts, 0, 1)


def unpack(packed_ref, s, slots):
    _, deep, _ = packed_ref.shape
    chunks = deep // slots
    parts = jnp.swapaxes(packed_ref[:, s * chunks : (s + 1) * chunks, :], 0, 1)
    return jnp.concatenate([parts[c] for c in range(chunks)], axis=1)


def place_kernel(routes_ref, gates_ref, grad_ref, out_ref, hot_ref):
    top, tokens = routes_ref.shape
    experts, _, _ = out_ref.shape
    rows = hot_ref.shape[0]
    row = lax.broadcasted_iota(jnp.int32, (rows, tokens), 0)
    number = row // experts
    named = row - number * experts
    slot = number.astype(F32)
    hits = jnp.zeros((rows, tokens), F32)
    gate = jnp.zeros((rows, tokens), F32)
    for k in range(top):
        hit = routes_ref[k : k + 1, :] == named
        hits = jnp.where(hit, 1.0, hits)
        gate = jnp.where(hit, gates_ref[k : k + 1, :], gate)
    before = (
        lax.broadcasted_iota(jnp.int32, (tokens, tokens), 0)
        < lax.broadcasted_iota(jnp.int32, (tokens, tokens), 1)
    ).astype(BF16)
    earlier = jnp.dot(hits.astype(BF16), before, preferred_element_type=F32)
    chosen = (hits > 0.5) & (jnp.abs(earlier - slot) < 0.5)
    weight = jnp.sum(jnp.where(chosen, gate, 0.0), axis=1, keepdims=True)
    hot = jnp.where(chosen, 1.0, 0.0).astype(BF16)
    hot_ref[...] = hot
    pack(weight * jnp.dot(hot, grad_ref[...], preferred_element_type=F32), out_ref)


def select_kernel(index_ref, gate_ref, up_ref, keep_ref, send_ref):
    slice_width = keep_ref.shape[3]
    for j in range(2 * LINKS):
        place = index_ref[j]
        low = j * slice_width
        parts = (gate_ref[:, low : low + slice_width], up_ref[:, low : low + slice_width])

        @pl.when(index_ref[2 * LINKS + j] == 1)
        def _():
            keep_ref[0, place] = parts[0]
            keep_ref[1, place] = parts[1]

        @pl.when(index_ref[2 * LINKS + j] == 0)
        def _():
            send_ref[0, place] = parts[0]
            send_ref[1, place] = parts[1]


def factor_kernel(saved_ref, gate_ref, up_ref):
    for p in range(LINKS):
        g = saved_ref[0, p].astype(F32)
        u = saved_ref[1, p].astype(F32)
        sig = jax.nn.sigmoid(g)
        up_ref[p] = g * sig
        gate_ref[p] = u * sig * (1.0 + g * (1.0 - sig))


def hidden_kernel(
    packed_ref, own_ref, left_ref, right_ref, far1_ref, far2_ref, gf_ref, uf_ref, gate_ref, up_ref, rows_ref
):
    slots = rows_ref.shape[0] // packed_ref.shape[0]
    for s in range(slots):
        rows_ref[s * packed_ref.shape[0] : (s + 1) * packed_ref.shape[0], :] = unpack(packed_ref, s, slots)

    def nt(a, b):
        return lax.dot_general(a, b, (((1,), (1,)), ((), ())), preferred_element_type=F32)

    half = far1_ref.shape[1]
    for p in range(LINKS):
        if p < 3:
            grad = nt(rows_ref[...], (own_ref, left_ref, right_ref)[p][...])
        else:
            grad = nt(rows_ref[:, :half], far1_ref[...]) + nt(rows_ref[:, half:], far2_ref[...])
        gate_ref[p] = (grad * gf_ref[p]).astype(BF16)
        up_ref[p] = (grad * uf_ref[p]).astype(BF16)


def output_kernel(gate_ref, up_ref, own_ref, left_ref, right_ref, farg_ref, faru_ref, *rest):
    out_ref = rest[-1]
    width = farg_ref.shape[0]

    def mm(a, b):
        return jnp.dot(a, b, preferred_element_type=F32)

    total = mm(gate_ref[3], farg_ref[...]) + mm(up_ref[3], faru_ref[...])
    for p, ref in enumerate((own_ref, left_ref, right_ref)):
        total += mm(gate_ref[p], ref[:width]) + mm(up_ref[p], ref[width:])
    if len(rest) == 2:
        total += rest[0][...].astype(F32)
    if len(out_ref.shape) == 3:
        pack(total, out_ref)
    else:
        out_ref[...] = total.astype(out_ref.dtype)


def turn_kernel(hot_ref, out_ref):
    out_ref[...] = hot_ref[...].T


def combine_kernel(hot_ref, *refs):
    out_ref = refs[-1]
    tokens, width = out_ref.shape
    half = width // 2
    for n, ref in enumerate(refs[:-1]):
        experts = ref.shape[0]
        slots = hot_ref.shape[1] // experts
        total = jnp.zeros((tokens, half), F32)
        for s in range(slots):
            total += jnp.dot(
                hot_ref[:, s * experts : (s + 1) * experts],
                unpack(ref, s, slots),
                preferred_element_type=F32,
            )
        out_ref[:, n * half : (n + 1) * half] = total.astype(BF16)


def body(grad_out, routes, gates, w_gate, w_up, w_down, saved_gate, saved_up):
    experts = lax.axis_size("expert")
    copies = lax.axis_size("replica")
    tokens, width = grad_out.shape
    slots = saved_gate.shape[3]
    slice_width = w_gate.shape[1]
    rows = experts * slots
    half = width // 2
    chunks = half // 128
    deep = slots * chunks
    replica = lax.axis_index("replica")
    link, core = replica // 2, replica % 2

    def along(a, by):
        pairs = [(2 * i + k, 2 * ((i + by) % LINKS) + k) for i in range(LINKS) for k in range(2)]
        return lax.ppermute(a, "replica", pairs)

    def across(a):
        return lax.ppermute(a, "replica", [(i, i ^ 1) for i in range(copies)])

    def exchange(a):
        return lax.all_to_all(a, "expert", split_axis=0, concat_axis=0, tiled=True)

    down = w_down[0]
    down_left, down_right = along(down, 1), along(down, -1)

    packed, hot = call(
        place_kernel,
        (routes.T, gates.T, grad_out),
        (
            jax.ShapeDtypeStruct((experts, 2 * deep, 128), BF16),
            jax.ShapeDtypeStruct((rows, tokens), BF16),
        ),
        2 * rows * tokens * width,
    )
    arrived = exchange(packed)

    first = jnp.concatenate([w_gate[0, :, :half], w_up[0, :, :half]], axis=0)
    second = jnp.concatenate([w_gate[0, :, half:], w_up[0, :, half:]], axis=0)
    first_left, first_right = along(first, 1), along(first, -1)
    down_far1 = along(down_left[:, :half], 1)
    down_far2 = along(down_right[:, half:], -1)
    second_left, second_right = along(second, 1), along(second, -1)
    first_farg = along(first_left[:slice_width], 1)
    first_faru = along(first_right[slice_width:], -1)
    second_farg = along(second_left[:slice_width], 1)
    second_faru = along(second_right[slice_width:], -1)

    order = jnp.arange(2 * LINKS, dtype=jnp.int32)
    offset = (order // 2 - link) & (LINKS - 1)
    where = jnp.where(offset == 0, 0, jnp.where(offset == 1, 2, jnp.where(offset == 2, 3, 1)))
    mine = (order % 2 == core).astype(jnp.int32)
    saved = tuple(a[0, 0].transpose(1, 0, 2).reshape(rows, -1) for a in (saved_gate, saved_up))
    piece = jax.ShapeDtypeStruct((2, LINKS, rows, slice_width), BF16)
    keep, send = call(select_kernel, (jnp.concatenate([where, mine]),) + saved, (piece, piece), smem=1)
    factor = jax.ShapeDtypeStruct((LINKS, rows, slice_width), F32)
    own_factors = call(factor_kernel, (keep,), (factor, factor))
    sent = across(send)
    other_factors = call(factor_kernel, (sent,), (factor, factor))

    downs = (down, down_left, down_right, down_far1, down_far2)
    hidden = jax.ShapeDtypeStruct((LINKS, rows, slice_width), BF16)
    cost = 2 * rows * LINKS * slice_width * width
    room = (pltpu.VMEM((rows, width), BF16),)
    other_rows = across(arrived)
    own_hidden = call(hidden_kernel, (arrived,) + downs + tuple(own_factors), (hidden, hidden), cost, scratch=room)
    other_hidden = call(
        hidden_kernel, (other_rows,) + downs + tuple(other_factors), (hidden, hidden), cost, scratch=room
    )

    results = []
    for pieces in (
        (first, first_left, first_right, first_farg, first_faru),
        (second, second_left, second_right, second_farg, second_faru),
    ):
        theirs = call(output_kernel, tuple(other_hidden) + pieces, (jax.ShapeDtypeStruct((rows, half), BF16),), cost)
        back = across(theirs)
        outgoing = call(
            output_kernel,
            tuple(own_hidden) + pieces + (back,),
            (jax.ShapeDtypeStruct((experts, deep, 128), BF16),),
            cost,
        )
        results.append(exchange(outgoing))
    turned = call(turn_kernel, (hot,), (jax.ShapeDtypeStruct((tokens, rows), BF16),))
    return call(combine_kernel, (turned,) + tuple(results), (jax.ShapeDtypeStruct((tokens, width), BF16),))


def solution(mesh):
    in_specs = (
        P(("expert", "replica"), None),
        P(("expert", "replica"), None),
        P(("expert", "replica"), None),
        P("expert", "replica", None),
        P("expert", "replica", None),
        P("expert", "replica", None),
        P("expert", "replica", None, None, None),
        P("expert", "replica", None, None, None),
    )
    out_specs = P(("expert", "replica"), None)

    return jax.shard_map(body, mesh=mesh, in_specs=in_specs, out_specs=out_specs, check_vma=False)
```

```python
import jax
import jax.numpy as jnp
from jax import lax
from jax.experimental import pallas as pl
from jax.experimental.pallas import tpu as pltpu
from jax.sharding import PartitionSpec as P

F32 = jnp.float32
BF16 = jnp.bfloat16
VM = pl.BlockSpec(memory_space=pltpu.VMEM)
SM = pl.BlockSpec(memory_space=pltpu.SMEM)
LINKS = 4


def call(kernel, ins, outs, flops=0, smem=0, scratch=(), spec=VM):
    moved = sum(a.size * a.dtype.itemsize for a in ins) + sum(o.size * o.dtype.itemsize for o in outs)
    single = len(outs) == 1
    return pl.pallas_call(
        kernel,
        out_shape=outs[0] if single else tuple(outs),
        in_specs=[SM] * smem + [spec] * (len(ins) - smem),
        out_specs=VM if single else tuple([VM] * len(outs)),
        scratch_shapes=list(scratch),
        cost_estimate=pl.CostEstimate(flops=flops, bytes_accessed=moved, transcendentals=0),
    )(*ins)


def fetch(copies, sems):
    made = [pltpu.make_async_copy(src, dst, sems.at[n]) for n, (src, dst) in enumerate(copies)]
    for copy in made:
        copy.start()
    return made


def pack(value, out_ref, part=0, parts=1):
    experts, deep, lanes = out_ref.shape
    slots = value.shape[0] // experts
    chunks = deep // slots
    span = chunks // parts
    for s in range(slots):
        block = value[s * experts : (s + 1) * experts].astype(BF16)
        stack = jnp.stack([block[:, c * lanes : (c + 1) * lanes] for c in range(span)])
        low = s * chunks + part * span
        out_ref[:, low : low + span, :] = jnp.swapaxes(stack, 0, 1)


def unpack(packed_ref, s, slots):
    _, deep, _ = packed_ref.shape
    chunks = deep // slots
    parts = jnp.swapaxes(packed_ref[:, s * chunks : (s + 1) * chunks, :], 0, 1)
    return jnp.concatenate([parts[c] for c in range(chunks)], axis=1)


def place_kernel(routes_ref, gates_ref, grad_ref, out_ref, hot_ref):
    top, tokens = routes_ref.shape
    experts, _, _ = out_ref.shape
    rows = hot_ref.shape[0]
    row = lax.broadcasted_iota(jnp.int32, (rows, tokens), 0)
    number = row // experts
    named = row - number * experts
    slot = number.astype(F32)
    hits = jnp.zeros((rows, tokens), F32)
    gate = jnp.zeros((rows, tokens), F32)
    for k in range(top):
        hit = routes_ref[k : k + 1, :] == named
        hits = jnp.where(hit, 1.0, hits)
        gate = jnp.where(hit, gates_ref[k : k + 1, :], gate)
    before = (
        lax.broadcasted_iota(jnp.int32, (tokens, tokens), 0)
        < lax.broadcasted_iota(jnp.int32, (tokens, tokens), 1)
    ).astype(BF16)
    earlier = jnp.dot(hits.astype(BF16), before, preferred_element_type=F32)
    chosen = (hits > 0.5) & (jnp.abs(earlier - slot) < 0.5)
    weight = jnp.sum(jnp.where(chosen, gate, 0.0), axis=1, keepdims=True)
    hot = jnp.where(chosen, 1.0, 0.0).astype(BF16)
    hot_ref[...] = hot
    pack(weight * jnp.dot(hot, grad_ref[...], preferred_element_type=F32), out_ref)


def factor_kernel(core_ref, gate_ref, up_ref, gf_ref, uf_ref):
    slice_width = gf_ref.shape[1] // LINKS
    first = core_ref[0] == 0
    for q in range(LINKS):
        low = 2 * q * slice_width
        mid, high = low + slice_width, low + 2 * slice_width
        g = jnp.where(first, gate_ref[:, low:mid].astype(F32), gate_ref[:, mid:high].astype(F32))
        u = jnp.where(first, up_ref[:, low:mid].astype(F32), up_ref[:, mid:high].astype(F32))
        sig = jax.nn.sigmoid(g)
        place = slice(q * slice_width, (q + 1) * slice_width)
        uf_ref[:, place] = g * sig
        gf_ref[:, place] = u * sig * (1.0 + g * (1.0 - sig))


def spots(link_ref, width):
    link = link_ref[0]
    steps = (0, LINKS - 1, 1, 2)
    return [pl.ds(pl.multiple_of(((link + by) & (LINKS - 1)) * width, 16), width) for by in steps]


def hidden_kernel(
    link_ref, packed_in, own_in, left_in, right_in, far1_in, far2_in, gf_in, uf_in,
    gate_ref, up_ref, packed_ref, down_ref, gf_ref, uf_ref, rows_ref, sems,
):
    width = own_in.shape[0]
    half = far1_in.shape[1]
    own, left, right, far = spots(link_ref, width)
    copies = fetch(
        [
            (packed_in, packed_ref),
            (own_in, down_ref.at[own, :]),
            (left_in, down_ref.at[left, :]),
            (right_in, down_ref.at[right, :]),
            (far1_in, down_ref.at[far, pl.ds(0, half)]),
            (far2_in, down_ref.at[far, pl.ds(half, half)]),
            (gf_in, gf_ref),
            (uf_in, uf_ref),
        ],
        sems,
    )
    copies[0].wait()
    experts = packed_ref.shape[0]
    slots = rows_ref.shape[0] // experts
    for s in range(slots):
        rows_ref[s * experts : (s + 1) * experts, :] = unpack(packed_ref, s, slots)
    for copy in copies[1:]:
        copy.wait()
    grad = lax.dot_general(
        rows_ref[...], down_ref[...], (((1,), (1,)), ((), ())), preferred_element_type=F32
    )
    gate_ref[...] = (grad * gf_ref[...]).astype(BF16)
    up_ref[...] = (grad * uf_ref[...]).astype(BF16)


def output_kernel(link_ref, gate_in, up_in, own_in, left_in, right_in, farg_in, faru_in, *rest):
    back_in = rest[0] if len(rest) == 7 else None
    out_ref, gate_ref, up_ref, weight_ref, back_ref, sems = rest[-6:]
    width = farg_in.shape[0]
    hidden = gate_in.shape[1]
    full = weight_ref.shape[1]
    span = full // 2
    own, left, right, far = spots(link_ref, width)
    small = [(gate_in, gate_ref), (up_in, up_ref)]
    if back_in is not None:
        small.append((back_in, back_ref))
    begun = fetch(small, sems.at[0])
    halves = []
    for n in range(2):
        columns = pl.ds(n * span, span)
        copies = []
        for piece, place in ((own_in, own), (left_in, left), (right_in, right)):
            copies.append((piece.at[pl.ds(0, width), columns], weight_ref.at[place, columns]))
            lower = pl.ds(pl.multiple_of(place.start + hidden, 16), width)
            copies.append((piece.at[pl.ds(width, width), columns], weight_ref.at[lower, columns]))
        copies.append((farg_in.at[:, columns], weight_ref.at[far, columns]))
        lower = pl.ds(pl.multiple_of(far.start + hidden, 16), width)
        copies.append((faru_in.at[:, columns], weight_ref.at[lower, columns]))
        halves.append(fetch(copies, sems.at[n + 1]))
    for copy in begun:
        copy.wait()
    for n in range(2):
        for copy in halves[n]:
            copy.wait()
        columns = slice(n * span, (n + 1) * span)
        total = jnp.dot(gate_ref[...], weight_ref[:hidden, columns], preferred_element_type=F32)
        total += jnp.dot(up_ref[...], weight_ref[hidden:, columns], preferred_element_type=F32)
        if back_in is None:
            out_ref[:, columns] = total.astype(out_ref.dtype)
        else:
            pack(total + back_ref[:, columns].astype(F32), out_ref, n, 2)


def turn_kernel(hot_ref, out_ref):
    out_ref[...] = hot_ref[...].T


def combine_kernel(hot_ref, back_ref, out_ref):
    tokens, width = out_ref.shape
    experts = back_ref.shape[0]
    slots = hot_ref.shape[1] // experts
    total = jnp.zeros((tokens, width), F32)
    for s in range(slots):
        total += jnp.dot(
            hot_ref[:, s * experts : (s + 1) * experts], unpack(back_ref, s, slots), preferred_element_type=F32
        )
    out_ref[...] = total.astype(BF16)


def body(grad_out, routes, gates, w_gate, w_up, w_down, saved_gate, saved_up):
    experts = lax.axis_size("expert")
    copies = lax.axis_size("replica")
    tokens, width = grad_out.shape
    slots = saved_gate.shape[3]
    slice_width = w_gate.shape[1]
    rows = experts * slots
    half = width // 2
    chunks = half // 128
    deep = slots * chunks
    replica = lax.axis_index("replica")

    def along(a, by):
        pairs = [(2 * i + k, 2 * ((i + by) % LINKS) + k) for i in range(LINKS) for k in range(2)]
        return lax.ppermute(a, "replica", pairs)

    def across(a):
        return lax.ppermute(a, "replica", [(i, i ^ 1) for i in range(copies)])

    def exchange(a):
        return lax.all_to_all(a, "expert", split_axis=0, concat_axis=0, tiled=True)

    down = w_down[0]
    down_left, down_right = along(down, 1), along(down, -1)

    packed, hot = call(
        place_kernel,
        (routes.T, gates.T, grad_out),
        (
            jax.ShapeDtypeStruct((experts, 2 * deep, 128), BF16),
            jax.ShapeDtypeStruct((rows, tokens), BF16),
        ),
        2 * rows * tokens * width,
    )
    arrived = exchange(packed)

    pair = jnp.concatenate([w_gate[0], w_up[0]], axis=0)
    pair_left, pair_right = along(pair, 1), along(pair, -1)
    down_far1 = along(down_left[:, :half], 1)
    down_far2 = along(down_right[:, half:], -1)
    for_right, for_left = pair_left[:slice_width], pair_right[slice_width:]
    pair_farg, pair_faru = along(for_right, 1), along(for_left, -1)

    link_at = (replica >> 1).reshape(1)
    core_at = (replica & 1).reshape(1)
    saved = tuple(a[0, 0].transpose(1, 0, 2).reshape(rows, -1) for a in (saved_gate, saved_up))
    hidden_units = LINKS * slice_width
    factor = jax.ShapeDtypeStruct((rows, hidden_units), F32)
    own_factors = call(factor_kernel, (core_at,) + saved, (factor, factor), smem=1)
    sent = (across(saved[0]), across(saved[1]))
    other_factors = call(factor_kernel, (core_at,) + sent, (factor, factor), smem=1)

    downs = (down, down_left, down_right, down_far1, down_far2)
    hidden = jax.ShapeDtypeStruct((rows, hidden_units), BF16)
    cost = 2 * rows * hidden_units * width
    scratch = (
        pltpu.VMEM((experts, 2 * deep, 128), BF16),
        pltpu.VMEM((hidden_units, width), BF16),
        pltpu.VMEM((rows, hidden_units), F32),
        pltpu.VMEM((rows, hidden_units), F32),
        pltpu.VMEM((rows, width), BF16),
        pltpu.SemaphoreType.DMA((8,)),
    )
    other_rows = across(arrived)

    def hide(packed_rows, factors):
        ins = (link_at, packed_rows) + downs + tuple(factors)
        return call(hidden_kernel, ins, (hidden, hidden), cost, 1, scratch, pl.BlockSpec(memory_space=pl.ANY))

    own_hidden = hide(arrived, own_factors)
    other_hidden = hide(other_rows, other_factors)

    pieces = (pair, pair_left, pair_right, pair_farg, pair_faru)
    scratch2 = (
        pltpu.VMEM((rows, hidden_units), BF16),
        pltpu.VMEM((rows, hidden_units), BF16),
        pltpu.VMEM((2 * hidden_units, width), BF16),
        pltpu.VMEM((rows, width), BF16),
        pltpu.SemaphoreType.DMA((3, 8)),
    )

    def give(grads, extra, out):
        ins = (link_at,) + tuple(grads) + pieces + extra
        return call(output_kernel, ins, (out,), 2 * cost, 1, scratch2, pl.BlockSpec(memory_space=pl.ANY))

    theirs = give(other_hidden, (), jax.ShapeDtypeStruct((rows, width), BF16))
    back = across(theirs)
    outgoing = give(own_hidden, (back,), jax.ShapeDtypeStruct((experts, 2 * deep, 128), BF16))
    returned = exchange(outgoing)
    turned = call(turn_kernel, (hot,), (jax.ShapeDtypeStruct((tokens, rows), BF16),))
    return call(combine_kernel, (turned, returned), (jax.ShapeDtypeStruct((tokens, width), BF16),))


def solution(mesh):
    in_specs = (
        P(("expert", "replica"), None),
        P(("expert", "replica"), None),
        P(("expert", "replica"), None),
        P("expert", "replica", None),
        P("expert", "replica", None),
        P("expert", "replica", None),
        P("expert", "replica", None, None, None),
        P("expert", "replica", None, None, None),
    )
    out_specs = P(("expert", "replica"), None)

    return jax.shard_map(body, mesh=mesh, in_specs=in_specs, out_specs=out_specs, check_vma=False)
```

```python
import jax
import jax.numpy as jnp
from jax import lax
from jax.experimental import pallas as pl
from jax.experimental.pallas import tpu as pltpu
from jax.sharding import PartitionSpec as P

F32 = jnp.float32
BF16 = jnp.bfloat16
VM = pl.BlockSpec(memory_space=pltpu.VMEM)
SM = pl.BlockSpec(memory_space=pltpu.SMEM)
LINKS = 4


def call(kernel, ins, outs, flops=0, smem=0, scratch=(), spec=VM, limit=24 << 20):
    moved = sum(a.size * a.dtype.itemsize for a in ins) + sum(o.size * o.dtype.itemsize for o in outs)
    single = len(outs) == 1
    return pl.pallas_call(
        kernel,
        out_shape=outs[0] if single else tuple(outs),
        in_specs=[SM] * smem + [spec] * (len(ins) - smem),
        out_specs=VM if single else tuple([VM] * len(outs)),
        scratch_shapes=list(scratch),
        compiler_params=pltpu.CompilerParams(vmem_limit_bytes=limit),
        cost_estimate=pl.CostEstimate(flops=flops, bytes_accessed=moved, transcendentals=0),
    )(*ins)


def fetch(copies, sems):
    made = [pltpu.make_async_copy(src, dst, sems.at[n]) for n, (src, dst) in enumerate(copies)]
    for copy in made:
        copy.start()
    return made


def pack(value, out_ref, part=0, parts=1):
    experts, deep, lanes = out_ref.shape
    slots = value.shape[0] // experts
    chunks = deep // slots
    span = chunks // parts
    for s in range(slots):
        block = value[s * experts : (s + 1) * experts].astype(BF16)
        stack = jnp.stack([block[:, c * lanes : (c + 1) * lanes] for c in range(span)])
        low = s * chunks + part * span
        out_ref[:, low : low + span, :] = jnp.swapaxes(stack, 0, 1)


def unpack(packed_ref, s, slots):
    _, deep, _ = packed_ref.shape
    chunks = deep // slots
    parts = jnp.swapaxes(packed_ref[:, s * chunks : (s + 1) * chunks, :], 0, 1)
    return jnp.concatenate([parts[c] for c in range(chunks)], axis=1)


def place_kernel(routes_ref, gates_ref, grad_ref, out_ref, hot_ref):
    top, tokens = routes_ref.shape
    experts, _, _ = out_ref.shape
    rows = hot_ref.shape[0]
    row = lax.broadcasted_iota(jnp.int32, (rows, tokens), 0)
    number = row // experts
    named = row - number * experts
    slot = number.astype(F32)
    hits = jnp.zeros((rows, tokens), F32)
    gate = jnp.zeros((rows, tokens), F32)
    for k in range(top):
        hit = routes_ref[k : k + 1, :] == named
        hits = jnp.where(hit, 1.0, hits)
        gate = jnp.where(hit, gates_ref[k : k + 1, :], gate)
    before = (
        lax.broadcasted_iota(jnp.int32, (tokens, tokens), 0)
        < lax.broadcasted_iota(jnp.int32, (tokens, tokens), 1)
    ).astype(BF16)
    earlier = jnp.dot(hits.astype(BF16), before, preferred_element_type=F32)
    chosen = (hits > 0.5) & (jnp.abs(earlier - slot) < 0.5)
    weight = jnp.sum(jnp.where(chosen, gate, 0.0), axis=1, keepdims=True)
    hot = jnp.where(chosen, 1.0, 0.0).astype(BF16)
    hot_ref[...] = hot
    pack(weight * jnp.dot(hot, grad_ref[...], preferred_element_type=F32), out_ref)


def factor_kernel(core_ref, gate_ref, up_ref, gf_ref, uf_ref):
    slice_width = gf_ref.shape[1] // LINKS
    first = core_ref[0] == 0
    for q in range(LINKS):
        low = 2 * q * slice_width
        mid, high = low + slice_width, low + 2 * slice_width
        g = jnp.where(first, gate_ref[:, low:mid].astype(F32), gate_ref[:, mid:high].astype(F32))
        u = jnp.where(first, up_ref[:, low:mid].astype(F32), up_ref[:, mid:high].astype(F32))
        sig = jax.nn.sigmoid(g)
        place = slice(q * slice_width, (q + 1) * slice_width)
        uf_ref[:, place] = g * sig
        gf_ref[:, place] = u * sig * (1.0 + g * (1.0 - sig))


def spots(link_ref, width):
    link = link_ref[0]
    steps = (0, LINKS - 1, 1, 2)
    return [pl.ds(pl.multiple_of(((link + by) & (LINKS - 1)) * width, 16), width) for by in steps]


def hidden_kernel(
    link_ref, packed_in, own_in, left_in, right_in, far_in, gf_in, uf_in,
    gate_ref, up_ref, packed_ref, down_ref, gf_ref, uf_ref, rows_ref, sems,
):
    width = own_in.shape[0]
    copies = [(packed_in, packed_ref)]
    for piece, place in zip((own_in, left_in, right_in, far_in), spots(link_ref, width)):
        copies.append((piece, down_ref.at[place, :]))
    copies = fetch(copies + [(gf_in, gf_ref), (uf_in, uf_ref)], sems)
    copies[0].wait()
    experts = packed_ref.shape[0]
    slots = rows_ref.shape[0] // experts
    for s in range(slots):
        rows_ref[s * experts : (s + 1) * experts, :] = unpack(packed_ref, s, slots)
    for copy in copies[1:]:
        copy.wait()
    grad = lax.dot_general(
        rows_ref[...], down_ref[...], (((1,), (1,)), ((), ())), preferred_element_type=F32
    )
    gate_ref[...] = (grad * gf_ref[...]).astype(BF16)
    up_ref[...] = (grad * uf_ref[...]).astype(BF16)


def output_kernel(
    link_ref, own_gate_in, own_up_in, other_gate_in, other_up_in, own_in, left_in, right_in, farg_in, faru_in,
    own_ref, theirs_ref, gate_ref, up_ref, weight_ref, sems,
):
    width = farg_in.shape[0]
    rows, hidden = own_gate_in.shape
    parts = sems.shape[0] - 1
    span = weight_ref.shape[1] // parts
    own, left, right, far = spots(link_ref, width)
    begun = fetch(
        [
            (own_gate_in, gate_ref.at[pl.ds(0, rows), :]),
            (own_up_in, up_ref.at[pl.ds(0, rows), :]),
            (other_gate_in, gate_ref.at[pl.ds(rows, rows), :]),
            (other_up_in, up_ref.at[pl.ds(rows, rows), :]),
        ],
        sems.at[0],
    )
    blocks = []
    for n in range(parts):
        columns = pl.ds(n * span, span)
        copies = []
        for piece, place in ((own_in, own), (left_in, left), (right_in, right)):
            copies.append((piece.at[pl.ds(0, width), columns], weight_ref.at[place, columns]))
            lower = pl.ds(pl.multiple_of(place.start + hidden, 16), width)
            copies.append((piece.at[pl.ds(width, width), columns], weight_ref.at[lower, columns]))
        copies.append((farg_in.at[:, columns], weight_ref.at[far, columns]))
        lower = pl.ds(pl.multiple_of(far.start + hidden, 16), width)
        copies.append((faru_in.at[:, columns], weight_ref.at[lower, columns]))
        blocks.append(fetch(copies, sems.at[n + 1]))
    for copy in begun:
        copy.wait()
    for n in range(parts):
        for copy in blocks[n]:
            copy.wait()
        columns = slice(n * span, (n + 1) * span)
        total = jnp.dot(gate_ref[...], weight_ref[:hidden, columns], preferred_element_type=F32)
        total += jnp.dot(up_ref[...], weight_ref[hidden:, columns], preferred_element_type=F32)
        own_ref[:, columns] = total[:rows].astype(BF16)
        theirs_ref[:, columns] = total[rows:].astype(BF16)


def join_kernel(own_ref, back_ref, out_ref):
    pack(own_ref[...].astype(F32) + back_ref[...].astype(F32), out_ref)


def turn_kernel(hot_ref, out_ref):
    out_ref[...] = hot_ref[...].T


def combine_kernel(hot_ref, back_ref, out_ref):
    tokens, width = out_ref.shape
    experts = back_ref.shape[0]
    slots = hot_ref.shape[1] // experts
    total = jnp.zeros((tokens, width), F32)
    for s in range(slots):
        total += jnp.dot(
            hot_ref[:, s * experts : (s + 1) * experts], unpack(back_ref, s, slots), preferred_element_type=F32
        )
    out_ref[...] = total.astype(BF16)


def body(grad_out, routes, gates, w_gate, w_up, w_down, saved_gate, saved_up):
    experts = lax.axis_size("expert")
    copies = lax.axis_size("replica")
    tokens, width = grad_out.shape
    slots = saved_gate.shape[3]
    slice_width = w_gate.shape[1]
    rows = experts * slots
    half = width // 2
    chunks = half // 128
    deep = slots * chunks
    replica = lax.axis_index("replica")

    def along(a, by):
        pairs = [(2 * i + k, 2 * ((i + by) % LINKS) + k) for i in range(LINKS) for k in range(2)]
        return lax.ppermute(a, "replica", pairs)

    def across(a):
        return lax.ppermute(a, "replica", [(i, i ^ 1) for i in range(copies)])

    def exchange(a):
        return lax.all_to_all(a, "expert", split_axis=0, concat_axis=0, tiled=True)

    down = w_down[0]
    down_left, down_right = along(down, 1), along(down, -1)

    packed, hot = call(
        place_kernel,
        (routes.T, gates.T, grad_out),
        (
            jax.ShapeDtypeStruct((experts, 2 * deep, 128), BF16),
            jax.ShapeDtypeStruct((rows, tokens), BF16),
        ),
        2 * rows * tokens * width,
    )
    arrived = exchange(packed)

    pair = jnp.concatenate([w_gate[0], w_up[0]], axis=0)
    pair_left, pair_right = along(pair, 1), along(pair, -1)
    down_far = along(down_left, 1)
    for_right, for_left = pair_left[:slice_width], pair_right[slice_width:]
    pair_farg, pair_faru = along(for_right, 1), along(for_left, -1)

    link_at = (replica >> 1).reshape(1)
    core_at = (replica & 1).reshape(1)
    saved = tuple(a[0, 0].transpose(1, 0, 2).reshape(rows, -1) for a in (saved_gate, saved_up))
    hidden_units = LINKS * slice_width
    factor = jax.ShapeDtypeStruct((rows, hidden_units), F32)
    own_factors = call(factor_kernel, (core_at,) + saved, (factor, factor), smem=1)
    sent = (across(saved[0]), across(saved[1]))
    other_factors = call(factor_kernel, (core_at,) + sent, (factor, factor), smem=1)

    downs = (down, down_left, down_right, down_far)
    hidden = jax.ShapeDtypeStruct((rows, hidden_units), BF16)
    cost = 2 * rows * hidden_units * width
    scratch = (
        pltpu.VMEM((experts, 2 * deep, 128), BF16),
        pltpu.VMEM((hidden_units, width), BF16),
        pltpu.VMEM((rows, hidden_units), F32),
        pltpu.VMEM((rows, hidden_units), F32),
        pltpu.VMEM((rows, width), BF16),
        pltpu.SemaphoreType.DMA((8,)),
    )
    other_rows = across(arrived)

    def hide(packed_rows, factors):
        ins = (link_at, packed_rows) + downs + tuple(factors)
        return call(hidden_kernel, ins, (hidden, hidden), cost, 1, scratch, pl.BlockSpec(memory_space=pl.ANY))

    own_hidden = hide(arrived, own_factors)
    other_hidden = hide(other_rows, other_factors)

    pieces = (pair, pair_left, pair_right, pair_farg, pair_faru)
    scratch2 = (
        pltpu.VMEM((2 * rows, hidden_units), BF16),
        pltpu.VMEM((2 * rows, hidden_units), BF16),
        pltpu.VMEM((2 * hidden_units, width), BF16),
        pltpu.SemaphoreType.DMA((5, 8)),
    )
    part = jax.ShapeDtypeStruct((rows, width), BF16)
    ours, theirs = call(
        output_kernel,
        (link_at,) + tuple(own_hidden) + tuple(other_hidden) + pieces,
        (part, part),
        4 * cost,
        1,
        scratch2,
        pl.BlockSpec(memory_space=pl.ANY),
    )
    back = across(theirs)
    outgoing = call(join_kernel, (ours, back), (jax.ShapeDtypeStruct((experts, 2 * deep, 128), BF16),))
    returned = exchange(outgoing)
    turned = call(turn_kernel, (hot,), (jax.ShapeDtypeStruct((tokens, rows), BF16),))
    return call(combine_kernel, (turned, returned), (jax.ShapeDtypeStruct((tokens, width), BF16),))


def solution(mesh):
    in_specs = (
        P(("expert", "replica"), None),
        P(("expert", "replica"), None),
        P(("expert", "replica"), None),
        P("expert", "replica", None),
        P("expert", "replica", None),
        P("expert", "replica", None),
        P("expert", "replica", None, None, None),
        P("expert", "replica", None, None, None),
    )
    out_specs = P(("expert", "replica"), None)

    return jax.shard_map(body, mesh=mesh, in_specs=in_specs, out_specs=out_specs, check_vma=False)
```

```python
import jax
import jax.numpy as jnp
from jax import lax
from jax.experimental import pallas as pl
from jax.experimental.pallas import tpu as pltpu
from jax.sharding import PartitionSpec as P

F32 = jnp.float32
BF16 = jnp.bfloat16
VM = pl.BlockSpec(memory_space=pltpu.VMEM)
SM = pl.BlockSpec(memory_space=pltpu.SMEM)
LINKS = 4
SLOTS = 3


def call(kernel, ins, outs, flops=0, smem=0, scratch=(), spec=VM, limit=24 << 20):
    moved = sum(a.size * a.dtype.itemsize for a in ins) + sum(o.size * o.dtype.itemsize for o in outs)
    single = len(outs) == 1
    return pl.pallas_call(
        kernel,
        out_shape=outs[0] if single else tuple(outs),
        in_specs=[SM] * smem + [spec] * (len(ins) - smem),
        out_specs=VM if single else tuple([VM] * len(outs)),
        scratch_shapes=list(scratch),
        compiler_params=pltpu.CompilerParams(vmem_limit_bytes=limit),
        cost_estimate=pl.CostEstimate(flops=flops, bytes_accessed=moved, transcendentals=0),
    )(*ins)


def fetch(copies, sems):
    made = [pltpu.make_async_copy(src, dst, sems.at[n]) for n, (src, dst) in enumerate(copies)]
    for copy in made:
        copy.start()
    return made


def pack(value, out_ref, part=0, parts=1):
    experts, deep, lanes = out_ref.shape
    slots = value.shape[0] // experts
    chunks = deep // slots
    span = chunks // parts
    for s in range(slots):
        block = value[s * experts : (s + 1) * experts].astype(BF16)
        stack = jnp.stack([block[:, c * lanes : (c + 1) * lanes] for c in range(span)])
        low = s * chunks + part * span
        out_ref[:, low : low + span, :] = jnp.swapaxes(stack, 0, 1)


def unpack(packed_ref, s, slots):
    _, deep, _ = packed_ref.shape
    chunks = deep // slots
    parts = jnp.swapaxes(packed_ref[:, s * chunks : (s + 1) * chunks, :], 0, 1)
    return jnp.concatenate([parts[c] for c in range(chunks)], axis=1)


def place_kernel(routes_ref, gates_ref, grad_ref, out_ref):
    top, tokens = routes_ref.shape
    experts, _, _ = out_ref.shape
    rows = experts * SLOTS
    row = lax.broadcasted_iota(jnp.int32, (rows, tokens), 0)
    number = row // experts
    named = row - number * experts
    slot = number.astype(F32)
    hits = jnp.zeros((rows, tokens), F32)
    gate = jnp.zeros((rows, tokens), F32)
    for k in range(top):
        hit = routes_ref[k : k + 1, :] == named
        hits = jnp.where(hit, 1.0, hits)
        gate = jnp.where(hit, gates_ref[k : k + 1, :], gate)
    before = (
        lax.broadcasted_iota(jnp.int32, (tokens, tokens), 0)
        < lax.broadcasted_iota(jnp.int32, (tokens, tokens), 1)
    ).astype(BF16)
    earlier = jnp.dot(hits.astype(BF16), before, preferred_element_type=F32)
    chosen = (hits > 0.5) & (jnp.abs(earlier - slot) < 0.5)
    weight = jnp.sum(jnp.where(chosen, gate, 0.0), axis=1, keepdims=True)
    hot = jnp.where(chosen, 1.0, 0.0).astype(BF16)
    pack(weight * jnp.dot(hot, grad_ref[...], preferred_element_type=F32), out_ref)


def factors(first, gate_ref, up_ref, gf_ref, uf_ref):
    slice_width = gf_ref.shape[1] // LINKS
    for q in range(LINKS):
        low = 2 * q * slice_width
        mid, high = low + slice_width, low + 2 * slice_width
        g = jnp.where(first, gate_ref[:, low:mid].astype(F32), gate_ref[:, mid:high].astype(F32))
        u = jnp.where(first, up_ref[:, low:mid].astype(F32), up_ref[:, mid:high].astype(F32))
        sig = jax.nn.sigmoid(g)
        place = slice(q * slice_width, (q + 1) * slice_width)
        uf_ref[:, place] = g * sig
        gf_ref[:, place] = u * sig * (1.0 + g * (1.0 - sig))


def spots(link_ref, width):
    link = link_ref[0]
    steps = (0, LINKS - 1, 1, 2)
    return [pl.ds(pl.multiple_of(((link + by) & (LINKS - 1)) * width, 16), width) for by in steps]


def hidden_kernel(
    link_ref, core_ref, packed_in, own_in, left_in, right_in, far_in, saved_gate_in, saved_up_in,
    gate_ref, up_ref, packed_ref, down_ref, saved_gate_ref, saved_up_ref, gf_ref, uf_ref, rows_ref, sems,
):
    width = own_in.shape[0]
    copies = [(saved_gate_in, saved_gate_ref), (saved_up_in, saved_up_ref), (packed_in, packed_ref)]
    for piece, place in zip((own_in, left_in, right_in, far_in), spots(link_ref, width)):
        copies.append((piece, down_ref.at[place, :]))
    copies = fetch(copies, sems)
    copies[0].wait()
    copies[1].wait()
    factors(core_ref[0] == 0, saved_gate_ref, saved_up_ref, gf_ref, uf_ref)
    copies[2].wait()
    experts = packed_ref.shape[0]
    slots = rows_ref.shape[0] // experts
    for s in range(slots):
        rows_ref[s * experts : (s + 1) * experts, :] = unpack(packed_ref, s, slots)
    for copy in copies[3:]:
        copy.wait()
    grad = lax.dot_general(
        rows_ref[...], down_ref[...], (((1,), (1,)), ((), ())), preferred_element_type=F32
    )
    gate_ref[...] = (grad * gf_ref[...]).astype(BF16)
    up_ref[...] = (grad * uf_ref[...]).astype(BF16)


def output_kernel(
    link_ref, own_gate_in, own_up_in, other_gate_in, other_up_in, own_in, left_in, right_in, far_in,
    own_ref, theirs_ref, gate_ref, up_ref, weight_ref, sems,
):
    width = own_in.shape[0] // 2
    rows, hidden = own_gate_in.shape
    parts = sems.shape[0] - 1
    span = weight_ref.shape[1] // parts
    own, left, right, far = spots(link_ref, width)
    begun = fetch(
        [
            (own_gate_in, gate_ref.at[pl.ds(0, rows), :]),
            (own_up_in, up_ref.at[pl.ds(0, rows), :]),
            (other_gate_in, gate_ref.at[pl.ds(rows, rows), :]),
            (other_up_in, up_ref.at[pl.ds(rows, rows), :]),
        ],
        sems.at[0],
    )
    blocks = []
    for n in range(parts):
        columns = pl.ds(n * span, span)
        copies = []
        for piece, place in ((own_in, own), (left_in, left), (right_in, right), (far_in, far)):
            copies.append((piece.at[pl.ds(0, width), columns], weight_ref.at[place, columns]))
            lower = pl.ds(pl.multiple_of(place.start + hidden, 16), width)
            copies.append((piece.at[pl.ds(width, width), columns], weight_ref.at[lower, columns]))
        blocks.append(fetch(copies, sems.at[n + 1]))
    for copy in begun:
        copy.wait()
    for n in range(parts):
        for copy in blocks[n]:
            copy.wait()
        columns = slice(n * span, (n + 1) * span)
        total = jnp.dot(gate_ref[...], weight_ref[:hidden, columns], preferred_element_type=F32)
        total += jnp.dot(up_ref[...], weight_ref[hidden:, columns], preferred_element_type=F32)
        own_ref[:, columns] = total[:rows].astype(BF16)
        theirs_ref[:, columns] = total[rows:].astype(BF16)


def join_kernel(own_ref, back_ref, out_ref):
    pack(own_ref[...].astype(F32) + back_ref[...].astype(F32), out_ref)


def turn_kernel(routes_ref, hot_ref):
    tokens, top = routes_ref.shape
    rows = hot_ref.shape[1]
    experts = rows // SLOTS
    row = lax.broadcasted_iota(jnp.int32, (tokens, rows), 1)
    number = row // experts
    named = row - number * experts
    slot = number.astype(F32)
    hits = jnp.zeros((tokens, rows), F32)
    for k in range(top):
        hits = jnp.where(routes_ref[:, k : k + 1] == named, 1.0, hits)
    before = (
        lax.broadcasted_iota(jnp.int32, (tokens, tokens), 1)
        < lax.broadcasted_iota(jnp.int32, (tokens, tokens), 0)
    ).astype(BF16)
    earlier = jnp.dot(before, hits.astype(BF16), preferred_element_type=F32)
    chosen = (hits > 0.5) & (jnp.abs(earlier - slot) < 0.5)
    hot_ref[...] = jnp.where(chosen, 1.0, 0.0).astype(BF16)


def combine_kernel(hot_ref, back_ref, out_ref):
    tokens, width = out_ref.shape
    experts = back_ref.shape[0]
    slots = hot_ref.shape[1] // experts
    total = jnp.zeros((tokens, width), F32)
    for s in range(slots):
        total += jnp.dot(
            hot_ref[:, s * experts : (s + 1) * experts], unpack(back_ref, s, slots), preferred_element_type=F32
        )
    out_ref[...] = total.astype(BF16)


def body(grad_out, routes, gates, w_gate, w_up, w_down, saved_gate, saved_up):
    experts = lax.axis_size("expert")
    copies = lax.axis_size("replica")
    tokens, width = grad_out.shape
    slots = saved_gate.shape[3]
    slice_width = w_gate.shape[1]
    rows = experts * slots
    half = width // 2
    chunks = half // 128
    deep = slots * chunks
    replica = lax.axis_index("replica")

    def along(a, by):
        pairs = [(2 * i + k, 2 * ((i + by) % LINKS) + k) for i in range(LINKS) for k in range(2)]
        return lax.ppermute(a, "replica", pairs)

    def across(a):
        return lax.ppermute(a, "replica", [(i, i ^ 1) for i in range(copies)])

    def exchange(a):
        return lax.all_to_all(a, "expert", split_axis=0, concat_axis=0, tiled=True)

    down = w_down[0]
    down_left, down_right = along(down, 1), along(down, -1)

    packed = call(
        place_kernel,
        (routes.T, gates.T, grad_out),
        (jax.ShapeDtypeStruct((experts, 2 * deep, 128), BF16),),
        2 * rows * tokens * width,
    )
    arrived = exchange(packed)

    pair = jnp.concatenate([w_gate[0], w_up[0]], axis=0)
    pair_left, pair_right = along(pair, 1), along(pair, -1)
    down_far = along(down_right, -1)
    pair_far = along(pair_left, 1)

    link_at = (replica >> 1).reshape(1)
    core_at = (replica & 1).reshape(1)
    saved = tuple(a[0, 0].transpose(1, 0, 2).reshape(rows, -1) for a in (saved_gate, saved_up))
    hidden_units = LINKS * slice_width
    sent = (across(saved[0]), across(saved[1]))

    downs = (down, down_left, down_right, down_far)
    hidden = jax.ShapeDtypeStruct((rows, hidden_units), BF16)
    cost = 2 * rows * hidden_units * width
    scratch = (
        pltpu.VMEM((experts, 2 * deep, 128), BF16),
        pltpu.VMEM((hidden_units, width), BF16),
        pltpu.VMEM(saved[0].shape, BF16),
        pltpu.VMEM(saved[0].shape, BF16),
        pltpu.VMEM((rows, hidden_units), F32),
        pltpu.VMEM((rows, hidden_units), F32),
        pltpu.VMEM((rows, width), BF16),
        pltpu.SemaphoreType.DMA((8,)),
    )
    other_rows = across(arrived)

    def hide(packed_rows, kept):
        ins = (link_at, core_at, packed_rows) + downs + tuple(kept)
        return call(hidden_kernel, ins, (hidden, hidden), cost, 2, scratch, pl.BlockSpec(memory_space=pl.ANY))

    own_hidden = hide(arrived, saved)
    other_hidden = hide(other_rows, sent)

    pieces = (pair, pair_left, pair_right, pair_far)
    scratch2 = (
        pltpu.VMEM((2 * rows, hidden_units), BF16),
        pltpu.VMEM((2 * rows, hidden_units), BF16),
        pltpu.VMEM((2 * hidden_units, width), BF16),
        pltpu.SemaphoreType.DMA((5, 8)),
    )
    part = jax.ShapeDtypeStruct((rows, width), BF16)
    ours, theirs = call(
        output_kernel,
        (link_at,) + tuple(own_hidden) + tuple(other_hidden) + pieces,
        (part, part),
        4 * cost,
        1,
        scratch2,
        pl.BlockSpec(memory_space=pl.ANY),
    )
    back = across(theirs)
    outgoing = call(join_kernel, (ours, back), (jax.ShapeDtypeStruct((experts, 2 * deep, 128), BF16),))
    returned = exchange(outgoing)
    turned = call(turn_kernel, (routes,), (jax.ShapeDtypeStruct((tokens, rows), BF16),))
    return call(combine_kernel, (turned, returned), (jax.ShapeDtypeStruct((tokens, width), BF16),))


def solution(mesh):
    in_specs = (
        P(("expert", "replica"), None),
        P(("expert", "replica"), None),
        P(("expert", "replica"), None),
        P("expert", "replica", None),
        P("expert", "replica", None),
        P("expert", "replica", None),
        P("expert", "replica", None, None, None),
        P("expert", "replica", None, None, None),
    )
    out_specs = P(("expert", "replica"), None)

    return jax.shard_map(body, mesh=mesh, in_specs=in_specs, out_specs=out_specs, check_vma=False)
```

```python
import jax
import jax.numpy as jnp
from jax import lax
from jax.experimental import pallas as pl
from jax.experimental.pallas import tpu as pltpu
from jax.sharding import PartitionSpec as P

F32 = jnp.float32
BF16 = jnp.bfloat16
VM = pl.BlockSpec(memory_space=pltpu.VMEM)
SM = pl.BlockSpec(memory_space=pltpu.SMEM)
LINKS = 4
SLOTS = 3


def call(kernel, ins, outs, flops=0, smem=0, scratch=(), spec=VM, limit=24 << 20):
    moved = sum(a.size * a.dtype.itemsize for a in ins) + sum(o.size * o.dtype.itemsize for o in outs)
    single = len(outs) == 1
    return pl.pallas_call(
        kernel,
        out_shape=outs[0] if single else tuple(outs),
        in_specs=[SM] * smem + [spec] * (len(ins) - smem),
        out_specs=VM if single else tuple([VM] * len(outs)),
        scratch_shapes=list(scratch),
        compiler_params=pltpu.CompilerParams(vmem_limit_bytes=limit),
        cost_estimate=pl.CostEstimate(flops=flops, bytes_accessed=moved, transcendentals=0),
    )(*ins)


def fetch(copies, sems):
    made = [pltpu.make_async_copy(src, dst, sems.at[n]) for n, (src, dst) in enumerate(copies)]
    for copy in made:
        copy.start()
    return made


def pack(value, out_ref, part=0, parts=1):
    experts, deep, lanes = out_ref.shape
    slots = value.shape[0] // experts
    chunks = deep // slots
    span = chunks // parts
    for s in range(slots):
        block = value[s * experts : (s + 1) * experts].astype(BF16)
        stack = jnp.stack([block[:, c * lanes : (c + 1) * lanes] for c in range(span)])
        low = s * chunks + part * span
        out_ref[:, low : low + span, :] = jnp.swapaxes(stack, 0, 1)


def unpack(packed_ref, s, slots):
    _, deep, _ = packed_ref.shape
    chunks = deep // slots
    parts = jnp.swapaxes(packed_ref[:, s * chunks : (s + 1) * chunks, :], 0, 1)
    return jnp.concatenate([parts[c] for c in range(chunks)], axis=1)


def place_kernel(routes_ref, gates_ref, grad_ref, out_ref):
    top, tokens = routes_ref.shape
    experts, _, _ = out_ref.shape
    rows = experts * SLOTS
    row = lax.broadcasted_iota(jnp.int32, (rows, tokens), 0)
    number = row // experts
    named = row - number * experts
    slot = number.astype(F32)
    hits = jnp.zeros((rows, tokens), F32)
    gate = jnp.zeros((rows, tokens), F32)
    for k in range(top):
        hit = routes_ref[k : k + 1, :] == named
        hits = jnp.where(hit, 1.0, hits)
        gate = jnp.where(hit, gates_ref[k : k + 1, :], gate)
    before = (
        lax.broadcasted_iota(jnp.int32, (tokens, tokens), 0)
        < lax.broadcasted_iota(jnp.int32, (tokens, tokens), 1)
    ).astype(BF16)
    earlier = jnp.dot(hits.astype(BF16), before, preferred_element_type=F32)
    chosen = (hits > 0.5) & (jnp.abs(earlier - slot) < 0.5)
    weight = jnp.sum(jnp.where(chosen, gate, 0.0), axis=1, keepdims=True)
    hot = jnp.where(chosen, 1.0, 0.0).astype(BF16)
    pack(weight * jnp.dot(hot, grad_ref[...], preferred_element_type=F32), out_ref)


def factors(first, gate_ref, up_ref, gf_ref, uf_ref):
    slice_width = gf_ref.shape[1] // LINKS
    for q in range(LINKS):
        low = 2 * q * slice_width
        mid, high = low + slice_width, low + 2 * slice_width
        g = jnp.where(first, gate_ref[:, low:mid].astype(F32), gate_ref[:, mid:high].astype(F32))
        u = jnp.where(first, up_ref[:, low:mid].astype(F32), up_ref[:, mid:high].astype(F32))
        sig = jax.nn.sigmoid(g)
        place = slice(q * slice_width, (q + 1) * slice_width)
        uf_ref[:, place] = g * sig
        gf_ref[:, place] = u * sig * (1.0 + g * (1.0 - sig))


def spots(link_ref, width):
    link = link_ref[0]
    steps = (0, LINKS - 1, 1, 2)
    return [pl.ds(pl.multiple_of(((link + by) & (LINKS - 1)) * width, 16), width) for by in steps]


def hidden_kernel(
    link_ref, core_ref, packed_in, own_in, left_in, right_in, far1_in, far2_in, saved_gate_in, saved_up_in,
    gate_ref, up_ref, packed_ref, down_ref, saved_gate_ref, saved_up_ref, gf_ref, uf_ref, rows_ref, sems,
):
    width = own_in.shape[0]
    copies = [(saved_gate_in, saved_gate_ref), (saved_up_in, saved_up_ref), (packed_in, packed_ref)]
    own, left, right, far = spots(link_ref, width)
    for piece, place in ((own_in, own), (left_in, left), (right_in, right)):
        copies.append((piece, down_ref.at[place, :]))
    cut = far1_in.shape[1]
    copies.append((far1_in, down_ref.at[far, pl.ds(0, cut)]))
    copies.append((far2_in, down_ref.at[far, pl.ds(cut, far2_in.shape[1])]))
    copies = fetch(copies, sems)
    copies[0].wait()
    copies[1].wait()
    factors(core_ref[0] == 0, saved_gate_ref, saved_up_ref, gf_ref, uf_ref)
    copies[2].wait()
    experts = packed_ref.shape[0]
    slots = rows_ref.shape[0] // experts
    for s in range(slots):
        rows_ref[s * experts : (s + 1) * experts, :] = unpack(packed_ref, s, slots)
    for copy in copies[3:]:
        copy.wait()
    grad = lax.dot_general(
        rows_ref[...], down_ref[...], (((1,), (1,)), ((), ())), preferred_element_type=F32
    )
    gate_ref[...] = (grad * gf_ref[...]).astype(BF16)
    up_ref[...] = (grad * uf_ref[...]).astype(BF16)


def output_kernel(
    link_ref, own_gate_in, own_up_in, other_gate_in, other_up_in,
    gate0_in, gate1_in, gate2_in, gate3_in, up0_in, up1_in, up2_in, up3_in,
    own_ref, theirs_ref, gate_ref, up_ref, weight_ref, sems,
):
    width = gate0_in.shape[0]
    rows, hidden = own_gate_in.shape
    parts = sems.shape[0] - 1
    span = weight_ref.shape[1] // parts
    places = spots(link_ref, width)
    gates, ups = (gate0_in, gate1_in, gate2_in, gate3_in), (up0_in, up1_in, up2_in, up3_in)
    begun = fetch(
        [
            (own_gate_in, gate_ref.at[pl.ds(0, rows), :]),
            (own_up_in, up_ref.at[pl.ds(0, rows), :]),
            (other_gate_in, gate_ref.at[pl.ds(rows, rows), :]),
            (other_up_in, up_ref.at[pl.ds(rows, rows), :]),
        ],
        sems.at[0],
    )
    blocks = []
    for n in range(parts):
        columns = pl.ds(n * span, span)
        copies = []
        for gate_in, up_in, place in zip(gates, ups, places):
            copies.append((gate_in.at[:, columns], weight_ref.at[place, columns]))
            lower = pl.ds(pl.multiple_of(place.start + hidden, 16), width)
            copies.append((up_in.at[:, columns], weight_ref.at[lower, columns]))
        blocks.append(fetch(copies, sems.at[n + 1]))
    for copy in begun:
        copy.wait()
    for n in range(parts):
        for copy in blocks[n]:
            copy.wait()
        columns = slice(n * span, (n + 1) * span)
        total = jnp.dot(gate_ref[...], weight_ref[:hidden, columns], preferred_element_type=F32)
        total += jnp.dot(up_ref[...], weight_ref[hidden:, columns], preferred_element_type=F32)
        own_ref[:, columns] = total[:rows].astype(BF16)
        theirs_ref[:, columns] = total[rows:].astype(BF16)


def join_kernel(own_ref, back_ref, out_ref):
    pack(own_ref[...].astype(F32) + back_ref[...].astype(F32), out_ref)


def turn_kernel(routes_ref, hot_ref):
    tokens, top = routes_ref.shape
    rows = hot_ref.shape[1]
    experts = rows // SLOTS
    row = lax.broadcasted_iota(jnp.int32, (tokens, rows), 1)
    number = row // experts
    named = row - number * experts
    slot = number.astype(F32)
    hits = jnp.zeros((tokens, rows), F32)
    for k in range(top):
        hits = jnp.where(routes_ref[:, k : k + 1] == named, 1.0, hits)
    before = (
        lax.broadcasted_iota(jnp.int32, (tokens, tokens), 1)
        < lax.broadcasted_iota(jnp.int32, (tokens, tokens), 0)
    ).astype(BF16)
    earlier = jnp.dot(before, hits.astype(BF16), preferred_element_type=F32)
    chosen = (hits > 0.5) & (jnp.abs(earlier - slot) < 0.5)
    hot_ref[...] = jnp.where(chosen, 1.0, 0.0).astype(BF16)


def combine_kernel(hot_ref, back_ref, out_ref):
    tokens, width = out_ref.shape
    experts = back_ref.shape[0]
    slots = hot_ref.shape[1] // experts
    total = jnp.zeros((tokens, width), F32)
    for s in range(slots):
        total += jnp.dot(
            hot_ref[:, s * experts : (s + 1) * experts], unpack(back_ref, s, slots), preferred_element_type=F32
        )
    out_ref[...] = total.astype(BF16)


def body(grad_out, routes, gates, w_gate, w_up, w_down, saved_gate, saved_up):
    experts = lax.axis_size("expert")
    copies = lax.axis_size("replica")
    tokens, width = grad_out.shape
    slots = saved_gate.shape[3]
    slice_width = w_gate.shape[1]
    rows = experts * slots
    half = width // 2
    chunks = half // 128
    deep = slots * chunks
    replica = lax.axis_index("replica")

    def along(a, by):
        pairs = [(2 * i + k, 2 * ((i + by) % LINKS) + k) for i in range(LINKS) for k in range(2)]
        return lax.ppermute(a, "replica", pairs)

    def across(a):
        return lax.ppermute(a, "replica", [(i, i ^ 1) for i in range(copies)])

    def exchange(a):
        return lax.all_to_all(a, "expert", split_axis=0, concat_axis=0, tiled=True)

    down = w_down[0]
    down_left, down_right = along(down, 1), along(down, -1)

    packed = call(
        place_kernel,
        (routes.T, gates.T, grad_out),
        (jax.ShapeDtypeStruct((experts, 2 * deep, 128), BF16),),
        2 * rows * tokens * width,
    )
    arrived = exchange(packed)

    gate, up = w_gate[0], w_up[0]
    gate_left, gate_right = along(gate, 1), along(gate, -1)
    up_left, up_right = along(up, 1), along(up, -1)
    cut = 3 * width // 4
    down_far1 = along(down_left[:, :cut], 1)
    down_far2 = along(down_right[:, cut:], -1)
    gate_far, up_far = along(gate_left, 1), along(up_right, -1)

    link_at = (replica >> 1).reshape(1)
    core_at = (replica & 1).reshape(1)
    saved = tuple(a[0, 0].transpose(1, 0, 2).reshape(rows, -1) for a in (saved_gate, saved_up))
    hidden_units = LINKS * slice_width
    sent = (across(saved[0]), across(saved[1]))

    downs = (down, down_left, down_right, down_far1, down_far2)
    hidden = jax.ShapeDtypeStruct((rows, hidden_units), BF16)
    cost = 2 * rows * hidden_units * width
    scratch = (
        pltpu.VMEM((experts, 2 * deep, 128), BF16),
        pltpu.VMEM((hidden_units, width), BF16),
        pltpu.VMEM(saved[0].shape, BF16),
        pltpu.VMEM(saved[0].shape, BF16),
        pltpu.VMEM((rows, hidden_units), F32),
        pltpu.VMEM((rows, hidden_units), F32),
        pltpu.VMEM((rows, width), BF16),
        pltpu.SemaphoreType.DMA((8,)),
    )
    other_rows = across(arrived)

    def hide(packed_rows, kept):
        ins = (link_at, core_at, packed_rows) + downs + tuple(kept)
        return call(hidden_kernel, ins, (hidden, hidden), cost, 2, scratch, pl.BlockSpec(memory_space=pl.ANY))

    own_hidden = hide(arrived, saved)
    other_hidden = hide(other_rows, sent)

    pieces = (gate, gate_left, gate_right, gate_far, up, up_left, up_right, up_far)
    scratch2 = (
        pltpu.VMEM((2 * rows, hidden_units), BF16),
        pltpu.VMEM((2 * rows, hidden_units), BF16),
        pltpu.VMEM((2 * hidden_units, width), BF16),
        pltpu.SemaphoreType.DMA((5, 8)),
    )
    part = jax.ShapeDtypeStruct((rows, width), BF16)
    ours, theirs = call(
        output_kernel,
        (link_at,) + tuple(own_hidden) + tuple(other_hidden) + pieces,
        (part, part),
        4 * cost,
        1,
        scratch2,
        pl.BlockSpec(memory_space=pl.ANY),
    )
    back = across(theirs)
    outgoing = call(join_kernel, (ours, back), (jax.ShapeDtypeStruct((experts, 2 * deep, 128), BF16),))
    returned = exchange(outgoing)
    turned = call(turn_kernel, (routes,), (jax.ShapeDtypeStruct((tokens, rows), BF16),))
    return call(combine_kernel, (turned, returned), (jax.ShapeDtypeStruct((tokens, width), BF16),))


def solution(mesh):
    in_specs = (
        P(("expert", "replica"), None),
        P(("expert", "replica"), None),
        P(("expert", "replica"), None),
        P("expert", "replica", None),
        P("expert", "replica", None),
        P("expert", "replica", None),
        P("expert", "replica", None, None, None),
        P("expert", "replica", None, None, None),
    )
    out_specs = P(("expert", "replica"), None)

    return jax.shard_map(body, mesh=mesh, in_specs=in_specs, out_specs=out_specs, check_vma=False)
```

```python
import jax
import jax.numpy as jnp
from jax import lax
from jax.experimental import pallas as pl
from jax.experimental.pallas import tpu as pltpu
from jax.sharding import PartitionSpec as P

F32 = jnp.float32
BF16 = jnp.bfloat16
VM = pl.BlockSpec(memory_space=pltpu.VMEM)
SM = pl.BlockSpec(memory_space=pltpu.SMEM)
LINKS = 4
SLOTS = 3


def call(kernel, ins, outs, flops=0, smem=0, scratch=(), spec=VM, limit=24 << 20):
    moved = sum(a.size * a.dtype.itemsize for a in ins) + sum(o.size * o.dtype.itemsize for o in outs)
    single = len(outs) == 1
    return pl.pallas_call(
        kernel,
        out_shape=outs[0] if single else tuple(outs),
        in_specs=[SM] * smem + [spec] * (len(ins) - smem),
        out_specs=VM if single else tuple([VM] * len(outs)),
        scratch_shapes=list(scratch),
        compiler_params=pltpu.CompilerParams(vmem_limit_bytes=limit),
        cost_estimate=pl.CostEstimate(flops=flops, bytes_accessed=moved, transcendentals=0),
    )(*ins)


def fetch(copies, sems):
    made = [pltpu.make_async_copy(src, dst, sems.at[n]) for n, (src, dst) in enumerate(copies)]
    for copy in made:
        copy.start()
    return made


def pack(value, out_ref, part=0, parts=1):
    experts, deep, lanes = out_ref.shape
    slots = value.shape[0] // experts
    chunks = deep // slots
    span = chunks // parts
    for s in range(slots):
        block = value[s * experts : (s + 1) * experts].astype(BF16)
        stack = jnp.stack([block[:, c * lanes : (c + 1) * lanes] for c in range(span)])
        low = s * chunks + part * span
        out_ref[:, low : low + span, :] = jnp.swapaxes(stack, 0, 1)


def unpack(packed_ref, s, slots):
    _, deep, _ = packed_ref.shape
    chunks = deep // slots
    parts = jnp.swapaxes(packed_ref[:, s * chunks : (s + 1) * chunks, :], 0, 1)
    return jnp.concatenate([parts[c] for c in range(chunks)], axis=1)


def place_kernel(routes_ref, gates_ref, grad_ref, out_ref):
    top, tokens = routes_ref.shape
    experts, _, _ = out_ref.shape
    rows = experts * SLOTS
    row = lax.broadcasted_iota(jnp.int32, (rows, tokens), 0)
    number = row // experts
    named = row - number * experts
    slot = number.astype(F32)
    hits = jnp.zeros((rows, tokens), F32)
    gate = jnp.zeros((rows, tokens), F32)
    for k in range(top):
        hit = routes_ref[k : k + 1, :] == named
        hits = jnp.where(hit, 1.0, hits)
        gate = jnp.where(hit, gates_ref[k : k + 1, :], gate)
    before = (
        lax.broadcasted_iota(jnp.int32, (tokens, tokens), 0)
        < lax.broadcasted_iota(jnp.int32, (tokens, tokens), 1)
    ).astype(BF16)
    earlier = jnp.dot(hits.astype(BF16), before, preferred_element_type=F32)
    chosen = (hits > 0.5) & (jnp.abs(earlier - slot) < 0.5)
    weight = jnp.sum(jnp.where(chosen, gate, 0.0), axis=1, keepdims=True)
    hot = jnp.where(chosen, 1.0, 0.0).astype(BF16)
    pack(weight * jnp.dot(hot, grad_ref[...], preferred_element_type=F32), out_ref)


def factors(first, gate_ref, up_ref, gf_ref, uf_ref):
    slice_width = gf_ref.shape[1] // LINKS
    for q in range(LINKS):
        low = 2 * q * slice_width
        mid, high = low + slice_width, low + 2 * slice_width
        g = jnp.where(first, gate_ref[:, low:mid].astype(F32), gate_ref[:, mid:high].astype(F32))
        u = jnp.where(first, up_ref[:, low:mid].astype(F32), up_ref[:, mid:high].astype(F32))
        sig = jax.nn.sigmoid(g)
        place = slice(q * slice_width, (q + 1) * slice_width)
        uf_ref[:, place] = g * sig
        gf_ref[:, place] = u * sig * (1.0 + g * (1.0 - sig))


def spots(link_ref, core_ref, width):
    link, turn = link_ref[0], 2 * core_ref[0] - 1
    steps = [(link + step * turn + LINKS) & (LINKS - 1) for step in range(LINKS)]
    return [pl.ds(pl.multiple_of(step * width, 16), width) for step in steps]


def hidden_kernel(
    link_ref, core_ref, packed_in, down0_in, down1_in, down2_in, down3_in, saved_gate_in, saved_up_in,
    gate_ref, up_ref, packed_ref, down_ref, saved_gate_ref, saved_up_ref, gf_ref, uf_ref, rows_ref, sems,
):
    width = down0_in.shape[0]
    copies = [(saved_gate_in, saved_gate_ref), (saved_up_in, saved_up_ref), (packed_in, packed_ref)]
    downs = (down0_in, down1_in, down2_in, down3_in)
    for piece, place in zip(downs, spots(link_ref, core_ref, width)):
        copies.append((piece, down_ref.at[place, :]))
    copies = fetch(copies, sems)
    copies[0].wait()
    copies[1].wait()
    factors(core_ref[0] == 0, saved_gate_ref, saved_up_ref, gf_ref, uf_ref)
    copies[2].wait()
    experts = packed_ref.shape[0]
    slots = rows_ref.shape[0] // experts
    for s in range(slots):
        rows_ref[s * experts : (s + 1) * experts, :] = unpack(packed_ref, s, slots)
    for copy in copies[3:]:
        copy.wait()
    grad = lax.dot_general(
        rows_ref[...], down_ref[...], (((1,), (1,)), ((), ())), preferred_element_type=F32
    )
    gate_ref[...] = (grad * gf_ref[...]).astype(BF16)
    up_ref[...] = (grad * uf_ref[...]).astype(BF16)


def output_kernel(
    link_ref, core_ref, own_gate_in, own_up_in, other_gate_in, other_up_in,
    gate0_in, gate1_in, gate2_in, gate3_in, up0_in, up1_in, up2_in, up3_in,
    own_ref, theirs_ref, gate_ref, up_ref, weight_ref, sems,
):
    width = gate0_in.shape[0]
    rows, hidden = own_gate_in.shape
    parts = sems.shape[0] - 1
    span = weight_ref.shape[1] // parts
    places = spots(link_ref, core_ref, width)
    gates, ups = (gate0_in, gate1_in, gate2_in, gate3_in), (up0_in, up1_in, up2_in, up3_in)
    begun = fetch(
        [
            (own_gate_in, gate_ref.at[pl.ds(0, rows), :]),
            (own_up_in, up_ref.at[pl.ds(0, rows), :]),
            (other_gate_in, gate_ref.at[pl.ds(rows, rows), :]),
            (other_up_in, up_ref.at[pl.ds(rows, rows), :]),
        ],
        sems.at[0],
    )
    blocks = []
    for n in range(parts):
        columns = pl.ds(n * span, span)
        copies = []
        for gate_in, up_in, place in zip(gates, ups, places):
            copies.append((gate_in.at[:, columns], weight_ref.at[place, columns]))
            lower = pl.ds(pl.multiple_of(place.start + hidden, 16), width)
            copies.append((up_in.at[:, columns], weight_ref.at[lower, columns]))
        blocks.append(fetch(copies, sems.at[n + 1]))
    for copy in begun:
        copy.wait()
    for n in range(parts):
        for copy in blocks[n]:
            copy.wait()
        columns = slice(n * span, (n + 1) * span)
        total = jnp.dot(gate_ref[...], weight_ref[:hidden, columns], preferred_element_type=F32)
        total += jnp.dot(up_ref[...], weight_ref[hidden:, columns], preferred_element_type=F32)
        own_ref[:, columns] = total[:rows].astype(BF16)
        theirs_ref[:, columns] = total[rows:].astype(BF16)


def join_kernel(own_ref, back_ref, out_ref):
    pack(own_ref[...].astype(F32) + back_ref[...].astype(F32), out_ref)


def turn_kernel(routes_ref, hot_ref):
    tokens, top = routes_ref.shape
    rows = hot_ref.shape[1]
    experts = rows // SLOTS
    row = lax.broadcasted_iota(jnp.int32, (tokens, rows), 1)
    number = row // experts
    named = row - number * experts
    slot = number.astype(F32)
    hits = jnp.zeros((tokens, rows), F32)
    for k in range(top):
        hits = jnp.where(routes_ref[:, k : k + 1] == named, 1.0, hits)
    before = (
        lax.broadcasted_iota(jnp.int32, (tokens, tokens), 1)
        < lax.broadcasted_iota(jnp.int32, (tokens, tokens), 0)
    ).astype(BF16)
    earlier = jnp.dot(before, hits.astype(BF16), preferred_element_type=F32)
    chosen = (hits > 0.5) & (jnp.abs(earlier - slot) < 0.5)
    hot_ref[...] = jnp.where(chosen, 1.0, 0.0).astype(BF16)


def combine_kernel(hot_ref, back_ref, out_ref):
    tokens, width = out_ref.shape
    experts = back_ref.shape[0]
    slots = hot_ref.shape[1] // experts
    total = jnp.zeros((tokens, width), F32)
    for s in range(slots):
        total += jnp.dot(
            hot_ref[:, s * experts : (s + 1) * experts], unpack(back_ref, s, slots), preferred_element_type=F32
        )
    out_ref[...] = total.astype(BF16)


def body(grad_out, routes, gates, w_gate, w_up, w_down, saved_gate, saved_up):
    experts = lax.axis_size("expert")
    copies = lax.axis_size("replica")
    tokens, width = grad_out.shape
    slots = saved_gate.shape[3]
    slice_width = w_gate.shape[1]
    rows = experts * slots
    half = width // 2
    chunks = half // 128
    deep = slots * chunks
    replica = lax.axis_index("replica")

    def along(a):
        pairs = [(2 * i + k, 2 * ((i + 1 - 2 * k) % LINKS) + k) for i in range(LINKS) for k in range(2)]
        return lax.ppermute(a, "replica", pairs)

    def across(a):
        return lax.ppermute(a, "replica", [(i, i ^ 1) for i in range(copies)])

    def exchange(a):
        return lax.all_to_all(a, "expert", split_axis=0, concat_axis=0, tiled=True)

    downs, gate_pieces, up_pieces = [w_down[0]], [w_gate[0]], [w_up[0]]
    for _ in range(1, LINKS):
        for pieces in (downs, gate_pieces, up_pieces):
            pieces.append(along(pieces[-1]))

    packed = call(
        place_kernel,
        (routes.T, gates.T, grad_out),
        (jax.ShapeDtypeStruct((experts, 2 * deep, 128), BF16),),
        2 * rows * tokens * width,
        limit=60 << 20,
    )
    arrived = exchange(packed)

    link_at = (replica >> 1).reshape(1)
    core_at = (replica & 1).reshape(1)
    saved = tuple(a[0, 0].transpose(1, 0, 2).reshape(rows, -1) for a in (saved_gate, saved_up))
    hidden_units = LINKS * slice_width
    sent = (across(saved[0]), across(saved[1]))

    hidden = jax.ShapeDtypeStruct((rows, hidden_units), BF16)
    cost = 2 * rows * hidden_units * width
    scratch = (
        pltpu.VMEM((experts, 2 * deep, 128), BF16),
        pltpu.VMEM((hidden_units, width), BF16),
        pltpu.VMEM(saved[0].shape, BF16),
        pltpu.VMEM(saved[0].shape, BF16),
        pltpu.VMEM((rows, hidden_units), F32),
        pltpu.VMEM((rows, hidden_units), F32),
        pltpu.VMEM((rows, width), BF16),
        pltpu.SemaphoreType.DMA((8,)),
    )
    other_rows = across(arrived)

    def hide(packed_rows, kept):
        ins = (link_at, core_at, packed_rows) + tuple(downs) + tuple(kept)
        return call(hidden_kernel, ins, (hidden, hidden), cost, 2, scratch, pl.BlockSpec(memory_space=pl.ANY))

    own_hidden = hide(arrived, saved)
    other_hidden = hide(other_rows, sent)

    pieces = tuple(gate_pieces + up_pieces)
    scratch2 = (
        pltpu.VMEM((2 * rows, hidden_units), BF16),
        pltpu.VMEM((2 * rows, hidden_units), BF16),
        pltpu.VMEM((2 * hidden_units, width), BF16),
        pltpu.SemaphoreType.DMA((5, 8)),
    )
    part = jax.ShapeDtypeStruct((rows, width), BF16)
    ours, theirs = call(
        output_kernel,
        (link_at, core_at) + tuple(own_hidden) + tuple(other_hidden) + pieces,
        (part, part),
        4 * cost,
        2,
        scratch2,
        pl.BlockSpec(memory_space=pl.ANY),
    )
    back = across(theirs)
    outgoing = call(join_kernel, (ours, back), (jax.ShapeDtypeStruct((experts, 2 * deep, 128), BF16),))
    returned = exchange(outgoing)
    turned = call(turn_kernel, (routes,), (jax.ShapeDtypeStruct((tokens, rows), BF16),))
    return call(combine_kernel, (turned, returned), (jax.ShapeDtypeStruct((tokens, width), BF16),))


def solution(mesh):
    in_specs = (
        P(("expert", "replica"), None),
        P(("expert", "replica"), None),
        P(("expert", "replica"), None),
        P("expert", "replica", None),
        P("expert", "replica", None),
        P("expert", "replica", None),
        P("expert", "replica", None, None, None),
        P("expert", "replica", None, None, None),
    )
    out_specs = P(("expert", "replica"), None)

    return jax.shard_map(body, mesh=mesh, in_specs=in_specs, out_specs=out_specs, check_vma=False)
```

```python
import jax
import jax.numpy as jnp
from jax import lax
from jax.experimental import pallas as pl
from jax.experimental.pallas import tpu as pltpu
from jax.sharding import PartitionSpec as P

F32 = jnp.float32
BF16 = jnp.bfloat16
VM = pl.BlockSpec(memory_space=pltpu.VMEM)
AN = pl.BlockSpec(memory_space=pl.ANY)
LINKS = 4
SLOTS = 3


def call(kernel, ins, outs, flops=0, scratch=(), spec=VM, limit=24 << 20):
    moved = sum(a.size * a.dtype.itemsize for a in ins) + sum(o.size * o.dtype.itemsize for o in outs)
    single = len(outs) == 1
    return pl.pallas_call(
        kernel,
        out_shape=outs[0] if single else tuple(outs),
        in_specs=[spec] * len(ins),
        out_specs=VM if single else tuple([VM] * len(outs)),
        scratch_shapes=list(scratch),
        compiler_params=pltpu.CompilerParams(vmem_limit_bytes=limit),
        cost_estimate=pl.CostEstimate(flops=flops, bytes_accessed=moved, transcendentals=0),
    )(*ins)


def fetch(copies, sems):
    made = [pltpu.make_async_copy(src, dst, sems.at[n]) for n, (src, dst) in enumerate(copies)]
    for copy in made:
        copy.start()
    return made


def pack(value, out_ref, part=0, parts=1):
    experts, deep, lanes = out_ref.shape
    slots = value.shape[0] // experts
    chunks = deep // slots
    span = chunks // parts
    for s in range(slots):
        block = value[s * experts : (s + 1) * experts].astype(BF16)
        stack = jnp.stack([block[:, c * lanes : (c + 1) * lanes] for c in range(span)])
        low = s * chunks + part * span
        out_ref[:, low : low + span, :] = jnp.swapaxes(stack, 0, 1)


def unpack(packed_ref, s, slots):
    _, deep, _ = packed_ref.shape
    chunks = deep // slots
    parts = jnp.swapaxes(packed_ref[:, s * chunks : (s + 1) * chunks, :], 0, 1)
    return jnp.concatenate([parts[c] for c in range(chunks)], axis=1)


def place_kernel(routes_ref, gates_ref, grad_ref, out_ref):
    named, chosen = chosen_of(routes_ref, out_ref.shape[0])
    weight = jnp.zeros(named.shape, F32)
    for k in range(routes_ref.shape[0]):
        weight = jnp.where(routes_ref[k : k + 1, :] == named, gates_ref[k : k + 1, :], weight)
    weight = jnp.sum(jnp.where(chosen, weight, 0.0), axis=1, keepdims=True)
    hot = jnp.where(chosen, 1.0, 0.0).astype(BF16)
    pack(weight * jnp.dot(hot, grad_ref[...], preferred_element_type=F32), out_ref)


def factor_kernel(gate_ref, up_ref, gf_ref, uf_ref):
    slice_width = gf_ref.shape[1] // LINKS
    first = (lax.axis_index("replica") & 1) == 0
    for q in range(LINKS):
        low = 2 * q * slice_width
        mid, high = low + slice_width, low + 2 * slice_width
        g = jnp.where(first, gate_ref[:, low:mid].astype(F32), gate_ref[:, mid:high].astype(F32))
        u = jnp.where(first, up_ref[:, low:mid].astype(F32), up_ref[:, mid:high].astype(F32))
        sig = jax.nn.sigmoid(g)
        place = slice(q * slice_width, (q + 1) * slice_width)
        uf_ref[:, place] = g * sig
        gf_ref[:, place] = u * sig * (1.0 + g * (1.0 - sig))


def spots(width):
    replica = lax.axis_index("replica")
    link, turn = replica >> 1, 2 * (replica & 1) - 1
    steps = [(link + step * turn + LINKS) & (LINKS - 1) for step in range(LINKS)]
    return [pl.ds(pl.multiple_of(step * width, 16), width) for step in steps]


def hidden_kernel(
    packed_in, down0_in, down1_in, down2_in, down3_in, gf_in, uf_in,
    hidden_ref, packed_ref, down_ref, gf_ref, uf_ref, rows_ref, sems,
):
    copies = [(packed_in, packed_ref)]
    for piece, place in zip((down0_in, down1_in, down2_in, down3_in), spots(down0_in.shape[0])):
        copies.append((piece, down_ref.at[place, :]))
    copies = fetch(copies + [(gf_in, gf_ref), (uf_in, uf_ref)], sems)
    copies[0].wait()
    experts = packed_ref.shape[0]
    slots = rows_ref.shape[0] // experts
    for s in range(slots):
        rows_ref[s * experts : (s + 1) * experts, :] = unpack(packed_ref, s, slots)
    for copy in copies[1:]:
        copy.wait()
    grad = lax.dot_general(
        rows_ref[...], down_ref[...], (((1,), (1,)), ((), ())), preferred_element_type=F32
    )
    units = grad.shape[1]
    hidden_ref[:, :units] = (grad * gf_ref[...]).astype(BF16)
    hidden_ref[:, units:] = (grad * uf_ref[...]).astype(BF16)


def output_kernel(
    own_in, other_in, gate0_in, gate1_in, gate2_in, gate3_in, up0_in, up1_in, up2_in, up3_in,
    own_ref, theirs_ref, hidden_ref, weight_ref, sems,
):
    width = gate0_in.shape[0]
    rows, hidden = own_in.shape[0], own_in.shape[1] // 2
    parts = sems.shape[0] - 1
    span = weight_ref.shape[1] // parts
    gates, ups = (gate0_in, gate1_in, gate2_in, gate3_in), (up0_in, up1_in, up2_in, up3_in)
    begun = fetch(
        [(own_in, hidden_ref.at[pl.ds(0, rows), :]), (other_in, hidden_ref.at[pl.ds(rows, rows), :])], sems.at[0]
    )
    blocks = []
    for n in range(parts):
        columns = pl.ds(n * span, span)
        copies = []
        for gate_in, up_in, place in zip(gates, ups, spots(width)):
            copies.append((gate_in.at[:, columns], weight_ref.at[place, columns]))
            lower = pl.ds(pl.multiple_of(place.start + hidden, 16), width)
            copies.append((up_in.at[:, columns], weight_ref.at[lower, columns]))
        blocks.append(fetch(copies, sems.at[n + 1]))
    for copy in begun:
        copy.wait()
    for n in range(parts):
        for copy in blocks[n]:
            copy.wait()
        columns = slice(n * span, (n + 1) * span)
        total = jnp.dot(hidden_ref[...], weight_ref[:, columns], preferred_element_type=F32)
        own_ref[:, columns] = total[:rows].astype(BF16)
        theirs_ref[:, columns] = total[rows:].astype(BF16)


def join_kernel(own_ref, back_ref, out_ref):
    pack(own_ref[...].astype(F32) + back_ref[...].astype(F32), out_ref)


def chosen_of(routes_ref, experts):
    top, tokens = routes_ref.shape
    row = lax.broadcasted_iota(jnp.int32, (experts * SLOTS, tokens), 0)
    number = row // experts
    named = row - number * experts
    hits = jnp.zeros(row.shape, F32)
    for k in range(top):
        hits = jnp.where(routes_ref[k : k + 1, :] == named, 1.0, hits)
    before = (
        lax.broadcasted_iota(jnp.int32, (tokens, tokens), 0)
        < lax.broadcasted_iota(jnp.int32, (tokens, tokens), 1)
    ).astype(BF16)
    earlier = jnp.dot(hits.astype(BF16), before, preferred_element_type=F32)
    return named, (hits > 0.5) & (jnp.abs(earlier - number.astype(F32)) < 0.5)


def turn_kernel(routes_ref, hot_ref):
    _, chosen = chosen_of(routes_ref, hot_ref.shape[1] // SLOTS)
    hot_ref[...] = jnp.where(chosen, 1.0, 0.0).T.astype(BF16)


def combine_kernel(hot_ref, back_ref, out_ref):
    tokens, width = out_ref.shape
    experts = back_ref.shape[0]
    slots = hot_ref.shape[1] // experts
    total = jnp.zeros((tokens, width), F32)
    for s in range(slots):
        total += jnp.dot(
            hot_ref[:, s * experts : (s + 1) * experts], unpack(back_ref, s, slots), preferred_element_type=F32
        )
    out_ref[...] = total.astype(BF16)


def body(grad_out, routes, gates, w_gate, w_up, w_down, saved_gate, saved_up):
    experts = lax.axis_size("expert")
    copies = lax.axis_size("replica")
    tokens, width = grad_out.shape
    slots = saved_gate.shape[3]
    slice_width = w_gate.shape[1]
    rows = experts * slots
    half = width // 2
    chunks = half // 128
    deep = slots * chunks

    def along(a):
        pairs = [(2 * i + k, 2 * ((i + 1 - 2 * k) % LINKS) + k) for i in range(LINKS) for k in range(2)]
        return lax.ppermute(a, "replica", pairs)

    def across(a):
        return lax.ppermute(a, "replica", [(i, i ^ 1) for i in range(copies)])

    def exchange(a):
        return lax.all_to_all(a, "expert", split_axis=0, concat_axis=0, tiled=True)

    downs, gate_pieces, up_pieces = [w_down[0]], [w_gate[0]], [w_up[0]]
    for _ in range(1, LINKS):
        for pieces in (downs, gate_pieces, up_pieces):
            pieces.append(along(pieces[-1]))

    packed = call(
        place_kernel,
        (routes.T, gates.T, grad_out),
        (jax.ShapeDtypeStruct((experts, 2 * deep, 128), BF16),),
        2 * rows * tokens * width,
        limit=60 << 20,
    )
    arrived = exchange(packed)

    saved = tuple(a[0, 0].transpose(1, 0, 2).reshape(rows, -1) for a in (saved_gate, saved_up))
    hidden_units = LINKS * slice_width
    factor = jax.ShapeDtypeStruct((rows, hidden_units), F32)
    own_factors = call(factor_kernel, saved, (factor, factor))
    sent = (across(saved[0]), across(saved[1]))
    other_factors = call(factor_kernel, sent, (factor, factor))

    hidden = jax.ShapeDtypeStruct((rows, 2 * hidden_units), BF16)
    cost = 2 * rows * hidden_units * width
    scratch = (
        pltpu.VMEM((experts, 2 * deep, 128), BF16),
        pltpu.VMEM((hidden_units, width), BF16),
        pltpu.VMEM((rows, hidden_units), F32),
        pltpu.VMEM((rows, hidden_units), F32),
        pltpu.VMEM((rows, width), BF16),
        pltpu.SemaphoreType.DMA((7,)),
    )
    other_rows = across(arrived)

    def hide(packed_rows, factors):
        ins = (packed_rows,) + tuple(downs) + tuple(factors)
        return call(hidden_kernel, ins, (hidden,), cost, scratch=scratch, spec=AN)

    own_hidden = hide(arrived, own_factors)
    other_hidden = hide(other_rows, other_factors)

    pieces = tuple(gate_pieces + up_pieces)
    scratch2 = (
        pltpu.VMEM((2 * rows, 2 * hidden_units), BF16),
        pltpu.VMEM((2 * hidden_units, width), BF16),
        pltpu.SemaphoreType.DMA((3, 8)),
    )
    part = jax.ShapeDtypeStruct((rows, width), BF16)
    ours, theirs = call(
        output_kernel, (own_hidden, other_hidden) + pieces, (part, part), 4 * cost, scratch=scratch2, spec=AN
    )
    back = across(theirs)
    outgoing = call(join_kernel, (ours, back), (jax.ShapeDtypeStruct((experts, 2 * deep, 128), BF16),))
    returned = exchange(outgoing)
    turned = call(turn_kernel, (routes.T,), (jax.ShapeDtypeStruct((tokens, rows), BF16),))
    return call(combine_kernel, (turned, returned), (jax.ShapeDtypeStruct((tokens, width), BF16),))


def solution(mesh):
    in_specs = (
        P(("expert", "replica"), None),
        P(("expert", "replica"), None),
        P(("expert", "replica"), None),
        P("expert", "replica", None),
        P("expert", "replica", None),
        P("expert", "replica", None),
        P("expert", "replica", None, None, None),
        P("expert", "replica", None, None, None),
    )
    out_specs = P(("expert", "replica"), None)

    return jax.shard_map(body, mesh=mesh, in_specs=in_specs, out_specs=out_specs, check_vma=False)
```

```python
import jax
import jax.numpy as jnp
from jax import lax
from jax.experimental import pallas as pl
from jax.experimental.pallas import tpu as pltpu
from jax.sharding import Mesh, PartitionSpec as P

F32 = jnp.float32
BF16 = jnp.bfloat16
VM = pl.BlockSpec(memory_space=pltpu.VMEM)
AN = pl.BlockSpec(memory_space=pl.ANY)
LINKS = 4
SLOTS = 3
ROWS_Y = 4


def call(kernel, ins, outs, flops=0, scratch=(), spec=VM, limit=24 << 20):
    moved = sum(a.size * a.dtype.itemsize for a in ins) + sum(o.size * o.dtype.itemsize for o in outs)
    single = len(outs) == 1
    return pl.pallas_call(
        kernel,
        out_shape=outs[0] if single else tuple(outs),
        in_specs=[spec] * len(ins),
        out_specs=VM if single else tuple([VM] * len(outs)),
        scratch_shapes=list(scratch),
        compiler_params=pltpu.CompilerParams(vmem_limit_bytes=limit),
        cost_estimate=pl.CostEstimate(flops=flops, bytes_accessed=moved, transcendentals=0),
    )(*ins)


def fetch(copies, sems):
    made = [pltpu.make_async_copy(src, dst, sems.at[n]) for n, (src, dst) in enumerate(copies)]
    for copy in made:
        copy.start()
    return made


def pack(value, out_ref, turned=False):
    experts, deep, lanes = out_ref.shape
    slots = value.shape[0] // experts
    chunks = deep // slots
    span = chunks
    for s in range(slots):
        block = value[s * experts : (s + 1) * experts].astype(BF16)
        stack = jnp.stack([block[:, c * lanes : (c + 1) * lanes] for c in range(span)])
        low = s * chunks
        blocks = jnp.swapaxes(stack, 0, 1)
        if not turned:
            out_ref[:, low : low + span, :] = blocks
            continue
        planes = experts // ROWS_Y
        blocks = blocks.reshape(planes, ROWS_Y, span, lanes)
        for y in range(ROWS_Y):
            out_ref[y * planes : (y + 1) * planes, low : low + span, :] = blocks[:, y]


def unpack(packed_ref, s, slots):
    _, deep, _ = packed_ref.shape
    chunks = deep // slots
    parts = jnp.swapaxes(packed_ref[:, s * chunks : (s + 1) * chunks, :], 0, 1)
    return jnp.concatenate([parts[c] for c in range(chunks)], axis=1)


def place_kernel(routes_ref, gates_ref, grad_ref, out_ref):
    named, chosen = chosen_of(routes_ref, out_ref.shape[0])
    weight = jnp.zeros(named.shape, F32)
    for k in range(routes_ref.shape[0]):
        weight = jnp.where(routes_ref[k : k + 1, :] == named, gates_ref[k : k + 1, :], weight)
    weight = jnp.sum(jnp.where(chosen, weight, 0.0), axis=1, keepdims=True)
    hot = jnp.where(chosen, 1.0, 0.0).astype(BF16)
    pack(weight * jnp.dot(hot, grad_ref[...], preferred_element_type=F32), out_ref)


def factor_kernel(gate_ref, up_ref, gf_ref, uf_ref):
    slice_width = gf_ref.shape[1] // LINKS
    first = (lax.axis_index("replica") & 1) == 0
    for q in range(LINKS):
        low = 2 * q * slice_width
        mid, high = low + slice_width, low + 2 * slice_width
        g = jnp.where(first, gate_ref[:, low:mid].astype(F32), gate_ref[:, mid:high].astype(F32))
        u = jnp.where(first, up_ref[:, low:mid].astype(F32), up_ref[:, mid:high].astype(F32))
        sig = jax.nn.sigmoid(g)
        place = slice(q * slice_width, (q + 1) * slice_width)
        uf_ref[:, place] = g * sig
        gf_ref[:, place] = u * sig * (1.0 + g * (1.0 - sig))


def spots(width):
    replica = lax.axis_index("replica")
    link, turn = replica >> 1, 2 * (replica & 1) - 1
    steps = [(link + step * turn + LINKS) & (LINKS - 1) for step in range(LINKS)]
    return [pl.ds(pl.multiple_of(step * width, 16), width) for step in steps]


def hidden_kernel(
    packed_in, down0_in, down1_in, down2_in, down3_in, gf_in, uf_in,
    hidden_ref, packed_ref, down_ref, gf_ref, uf_ref, rows_ref, sems,
):
    planes, across_y, deep, lanes = packed_ref.shape
    copies = [(packed_in.at[pl.ds(y * planes, planes)], packed_ref.at[:, y]) for y in range(across_y)]
    half = down_ref.shape[1] // 2
    downs = (down0_in, down1_in, down2_in, down3_in)
    for n in range(2):
        columns = pl.ds(n * half, half)
        for piece, place in zip(downs, spots(down0_in.shape[0])):
            copies.append((piece.at[:, columns], down_ref.at[place, columns]))
    copies = fetch(copies + [(gf_in, gf_ref), (uf_in, uf_ref)], sems)
    for copy in copies[:across_y]:
        copy.wait()
    experts = planes * across_y
    slots = rows_ref.shape[0] // experts
    packed = packed_ref[...].reshape(experts, deep, lanes)
    for s in range(slots):
        rows_ref[s * experts : (s + 1) * experts, :] = unpack(packed, s, slots)
    grad = jnp.zeros(gf_ref.shape, F32)
    for n in range(2):
        for copy in copies[across_y + n * LINKS : across_y + (n + 1) * LINKS]:
            copy.wait()
        columns = slice(n * half, (n + 1) * half)
        grad += lax.dot_general(
            rows_ref[:, columns], down_ref[:, columns], (((1,), (1,)), ((), ())), preferred_element_type=F32
        )
    for copy in copies[across_y + 2 * LINKS :]:
        copy.wait()
    units = grad.shape[1]
    hidden_ref[:, :units] = (grad * gf_ref[...]).astype(BF16)
    hidden_ref[:, units:] = (grad * uf_ref[...]).astype(BF16)


def output_kernel(
    own_in, other_in, gate0_in, gate1_in, gate2_in, gate3_in, up0_in, up1_in, up2_in, up3_in,
    own_ref, theirs_ref, hidden_ref, weight_ref, sems,
):
    width = gate0_in.shape[0]
    rows, hidden = own_in.shape[0], own_in.shape[1] // 2
    parts = sems.shape[0] - 1
    span = weight_ref.shape[1] // parts
    gates, ups = (gate0_in, gate1_in, gate2_in, gate3_in), (up0_in, up1_in, up2_in, up3_in)
    begun = fetch(
        [(own_in, hidden_ref.at[pl.ds(0, rows), :]), (other_in, hidden_ref.at[pl.ds(rows, rows), :])], sems.at[0]
    )
    blocks = []
    for n in range(parts):
        columns = pl.ds(n * span, span)
        copies = []
        for gate_in, up_in, place in zip(gates, ups, spots(width)):
            copies.append((gate_in.at[:, columns], weight_ref.at[place, columns]))
            lower = pl.ds(pl.multiple_of(place.start + hidden, 16), width)
            copies.append((up_in.at[:, columns], weight_ref.at[lower, columns]))
        blocks.append(fetch(copies, sems.at[n + 1]))
    for copy in begun:
        copy.wait()
    for n in range(parts):
        for copy in blocks[n]:
            copy.wait()
        columns = slice(n * span, (n + 1) * span)
        total = jnp.dot(hidden_ref[...], weight_ref[:, columns], preferred_element_type=F32)
        own_ref[:, columns] = total[:rows].astype(BF16)
        theirs_ref[:, columns] = total[rows:].astype(BF16)


def join_kernel(own_ref, back_ref, out_ref):
    pack(own_ref[...].astype(F32) + back_ref[...].astype(F32), out_ref, True)


def chosen_of(routes_ref, experts):
    top, tokens = routes_ref.shape
    row = lax.broadcasted_iota(jnp.int32, (experts * SLOTS, tokens), 0)
    number = row // experts
    block = row - number * experts
    planes = experts // ROWS_Y
    named = (block % planes) * ROWS_Y + block // planes
    hits = jnp.zeros(row.shape, F32)
    for k in range(top):
        hits = jnp.where(routes_ref[k : k + 1, :] == named, 1.0, hits)
    before = (
        lax.broadcasted_iota(jnp.int32, (tokens, tokens), 0)
        < lax.broadcasted_iota(jnp.int32, (tokens, tokens), 1)
    ).astype(BF16)
    earlier = jnp.dot(hits.astype(BF16), before, preferred_element_type=F32)
    return named, (hits > 0.5) & (jnp.abs(earlier - number.astype(F32)) < 0.5)


def turn_kernel(routes_ref, hot_ref):
    _, chosen = chosen_of(routes_ref, hot_ref.shape[1] // SLOTS)
    hot_ref[...] = jnp.where(chosen, 1.0, 0.0).T.astype(BF16)


def combine_kernel(hot_ref, back_ref, out_ref):
    tokens, width = out_ref.shape
    experts = back_ref.shape[0]
    slots = hot_ref.shape[1] // experts
    total = jnp.zeros((tokens, width), F32)
    for s in range(slots):
        total += jnp.dot(
            hot_ref[:, s * experts : (s + 1) * experts], unpack(back_ref, s, slots), preferred_element_type=F32
        )
    out_ref[...] = total.astype(BF16)


def body(grad_out, routes, gates, w_gate, w_up, w_down, saved_gate, saved_up):
    experts = lax.axis_size("z") * lax.axis_size("y")
    copies = lax.axis_size("replica")
    tokens, width = grad_out.shape
    slots = saved_gate.shape[3]
    slice_width = w_gate.shape[1]
    rows = experts * slots
    half = width // 2
    chunks = half // 128
    deep = slots * chunks

    def along(a):
        pairs = [(2 * i + k, 2 * ((i + 1 - 2 * k) % LINKS) + k) for i in range(LINKS) for k in range(2)]
        return lax.ppermute(a, "replica", pairs)

    def across(a):
        return lax.ppermute(a, "replica", [(i, i ^ 1) for i in range(copies)])

    def exchange(a):
        return lax.all_to_all(a, ("y", "z"), split_axis=0, concat_axis=0, tiled=True)

    downs, gate_pieces, up_pieces = [w_down[0]], [w_gate[0]], [w_up[0]]
    for _ in range(1, LINKS):
        for pieces in (downs, gate_pieces, up_pieces):
            pieces.append(along(pieces[-1]))

    packed = call(
        place_kernel,
        (routes.T, gates.T, grad_out),
        (jax.ShapeDtypeStruct((experts, 2 * deep, 128), BF16),),
        2 * rows * tokens * width,
        limit=60 << 20,
    )
    arrived = exchange(packed)

    saved = tuple(a[0, 0].transpose(1, 0, 2).reshape(rows, -1) for a in (saved_gate, saved_up))
    hidden_units = LINKS * slice_width
    factor = jax.ShapeDtypeStruct((rows, hidden_units), F32)
    own_factors = call(factor_kernel, saved, (factor, factor))
    sent = (across(saved[0]), across(saved[1]))
    other_factors = call(factor_kernel, sent, (factor, factor))

    hidden = jax.ShapeDtypeStruct((rows, 2 * hidden_units), BF16)
    cost = 2 * rows * hidden_units * width
    scratch = (
        pltpu.VMEM((experts // ROWS_Y, ROWS_Y, 2 * deep, 128), BF16),
        pltpu.VMEM((hidden_units, width), BF16),
        pltpu.VMEM((rows, hidden_units), F32),
        pltpu.VMEM((rows, hidden_units), F32),
        pltpu.VMEM((rows, width), BF16),
        pltpu.SemaphoreType.DMA((ROWS_Y + 2 * LINKS + 2,)),
    )
    other_rows = across(arrived)

    def hide(packed_rows, factors):
        ins = (packed_rows,) + tuple(downs) + tuple(factors)
        return call(hidden_kernel, ins, (hidden,), cost, scratch=scratch, spec=AN)

    own_hidden = hide(arrived, own_factors)
    other_hidden = hide(other_rows, other_factors)

    pieces = tuple(gate_pieces + up_pieces)
    scratch2 = (
        pltpu.VMEM((2 * rows, 2 * hidden_units), BF16),
        pltpu.VMEM((2 * hidden_units, width), BF16),
        pltpu.SemaphoreType.DMA((3, 8)),
    )
    part = jax.ShapeDtypeStruct((rows, width), BF16)
    ours, theirs = call(
        output_kernel, (own_hidden, other_hidden) + pieces, (part, part), 4 * cost, scratch=scratch2, spec=AN
    )
    back = across(theirs)
    outgoing = call(join_kernel, (ours, back), (jax.ShapeDtypeStruct((experts, 2 * deep, 128), BF16),))
    returned = exchange(outgoing)
    turned = call(turn_kernel, (routes.T,), (jax.ShapeDtypeStruct((tokens, rows), BF16),))
    return call(combine_kernel, (turned, returned), (jax.ShapeDtypeStruct((tokens, width), BF16),))


def solution(mesh):
    devices = mesh.devices
    split = Mesh(devices.reshape(-1, ROWS_Y, devices.shape[1]), ("z", "y", "replica"))
    in_specs = (
        P(("z", "y", "replica"), None),
        P(("z", "y", "replica"), None),
        P(("z", "y", "replica"), None),
        P(("z", "y"), "replica", None),
        P(("z", "y"), "replica", None),
        P(("z", "y"), "replica", None),
        P(("z", "y"), "replica", None, None, None),
        P(("z", "y"), "replica", None, None, None),
    )
    out_specs = P(("z", "y", "replica"), None)

    return jax.shard_map(body, mesh=split, in_specs=in_specs, out_specs=out_specs, check_vma=False)
```

```python
import jax
import jax.numpy as jnp
from jax import lax
from jax.experimental import pallas as pl
from jax.experimental.pallas import tpu as pltpu
from jax.sharding import Mesh, PartitionSpec as P

F32 = jnp.float32
BF16 = jnp.bfloat16
VM = pl.BlockSpec(memory_space=pltpu.VMEM)
AN = pl.BlockSpec(memory_space=pl.ANY)
LINKS = 4
SLOTS = 3
ROWS_Y = 4


def call(kernel, ins, outs, flops=0, scratch=(), spec=VM, limit=24 << 20):
    moved = sum(a.size * a.dtype.itemsize for a in ins) + sum(o.size * o.dtype.itemsize for o in outs)
    single = len(outs) == 1
    return pl.pallas_call(
        kernel,
        out_shape=outs[0] if single else tuple(outs),
        in_specs=spec if isinstance(spec, list) else [spec] * len(ins),
        out_specs=VM if single else tuple([VM] * len(outs)),
        scratch_shapes=list(scratch),
        compiler_params=pltpu.CompilerParams(vmem_limit_bytes=limit),
        cost_estimate=pl.CostEstimate(flops=flops, bytes_accessed=moved, transcendentals=0),
    )(*ins)


def fetch(copies, sems):
    made = [pltpu.make_async_copy(src, dst, sems.at[n]) for n, (src, dst) in enumerate(copies)]
    for copy in made:
        copy.start()
    return made


def pack(value, out_ref, turned=False):
    experts, deep, lanes = out_ref.shape
    slots = value.shape[0] // experts
    chunks = deep // slots
    span = chunks
    for s in range(slots):
        block = value[s * experts : (s + 1) * experts].astype(BF16)
        stack = jnp.stack([block[:, c * lanes : (c + 1) * lanes] for c in range(span)])
        low = s * chunks
        blocks = jnp.swapaxes(stack, 0, 1)
        if not turned:
            out_ref[:, low : low + span, :] = blocks
            continue
        planes = experts // ROWS_Y
        blocks = blocks.reshape(planes, ROWS_Y, span, lanes)
        for y in range(ROWS_Y):
            out_ref[y * planes : (y + 1) * planes, low : low + span, :] = blocks[:, y]


def unpack(packed_ref, s, slots):
    _, deep, _ = packed_ref.shape
    chunks = deep // slots
    parts = jnp.swapaxes(packed_ref[:, s * chunks : (s + 1) * chunks, :], 0, 1)
    return jnp.concatenate([parts[c] for c in range(chunks)], axis=1)


def place_kernel(routes_ref, gates_ref, grad_ref, out_ref):
    named, chosen = chosen_of(routes_ref, out_ref.shape[0])
    weight = jnp.zeros(named.shape, F32)
    for k in range(routes_ref.shape[0]):
        weight = jnp.where(routes_ref[k : k + 1, :] == named, gates_ref[k : k + 1, :], weight)
    weight = jnp.sum(jnp.where(chosen, weight, 0.0), axis=1, keepdims=True)
    hot = jnp.where(chosen, 1.0, 0.0).astype(BF16)
    pack(weight * jnp.dot(hot, grad_ref[...], preferred_element_type=F32), out_ref)


def factor_kernel(gate_ref, up_ref, gf_ref, uf_ref):
    slice_width = gf_ref.shape[2]
    replica = lax.axis_index("replica")
    link, turn = replica >> 1, 2 * (replica & 1) - 1
    first = turn < 0
    for q in range(LINKS):
        low = 2 * q * slice_width
        mid, high = low + slice_width, low + 2 * slice_width
        g = jnp.where(first, gate_ref[:, low:mid].astype(F32), gate_ref[:, mid:high].astype(F32))
        u = jnp.where(first, up_ref[:, low:mid].astype(F32), up_ref[:, mid:high].astype(F32))
        sig = jax.nn.sigmoid(g)
        step = ((q - link) * turn + 2 * LINKS) & (LINKS - 1)
        uf_ref[step] = g * sig
        gf_ref[step] = u * sig * (1.0 + g * (1.0 - sig))


def hidden_kernel(
    packed_in, down0_in, down1_in, down2_in, down3_in, gf_in, uf_in,
    early_ref, late_ref, packed_ref, down_ref, gf_ref, uf_ref, rows_ref, sems,
):
    planes, across_y, deep, lanes = packed_ref.shape
    copies = [(packed_in.at[pl.ds(y * planes, planes)], packed_ref.at[:, y]) for y in range(across_y)]
    half = down_ref.shape[1] // 2
    width = down0_in.shape[0]
    downs = (down0_in, down1_in, down2_in, down3_in)
    for n in range(2):
        columns = pl.ds(n * half, half)
        for step, piece in enumerate(downs):
            place = pl.ds(step * width, width)
            copies.append((piece.at[:, columns], down_ref.at[place, columns]))
    copies = fetch(copies + [(gf_in, gf_ref), (uf_in, uf_ref)], sems)
    for copy in copies[:across_y]:
        copy.wait()
    experts = planes * across_y
    slots = rows_ref.shape[0] // experts
    packed = packed_ref[...].reshape(experts, deep, lanes)
    for s in range(slots):
        rows_ref[s * experts : (s + 1) * experts, :] = unpack(packed, s, slots)
    grad = jnp.zeros((rows_ref.shape[0], down_ref.shape[0]), F32)
    for n in range(2):
        for copy in copies[across_y + n * LINKS : across_y + (n + 1) * LINKS]:
            copy.wait()
        columns = slice(n * half, (n + 1) * half)
        grad += lax.dot_general(
            rows_ref[:, columns], down_ref[:, columns], (((1,), (1,)), ((), ())), preferred_element_type=F32
        )
    for copy in copies[across_y + 2 * LINKS :]:
        copy.wait()
    for step in range(LINKS):
        part = grad[:, step * width : (step + 1) * width]
        out_ref, low = (early_ref, 2 * step * width) if step < LINKS - 1 else (late_ref, 0)
        out_ref[:, low : low + width] = (part * gf_ref[step]).astype(BF16)
        out_ref[:, low + width : low + 2 * width] = (part * uf_ref[step]).astype(BF16)


def gather(own_in, other_in, pieces, hidden_ref, weight_ref, sems):
    rows, width = own_in.shape[0], pieces[0].shape[0]
    parts = sems.shape[0] - 1
    span = weight_ref.shape[1] // parts
    begun = fetch(
        [(own_in, hidden_ref.at[pl.ds(0, rows), :]), (other_in, hidden_ref.at[pl.ds(rows, rows), :])], sems.at[0]
    )
    blocks = []
    for n in range(parts):
        columns = pl.ds(n * span, span)
        copies = [
            (piece.at[:, columns], weight_ref.at[pl.ds(k * width, width), columns]) for k, piece in enumerate(pieces)
        ]
        blocks.append(fetch(copies, sems.at[n + 1]))
    for copy in begun:
        copy.wait()
    for n in range(parts):
        for copy in blocks[n]:
            copy.wait()
        columns = slice(n * span, (n + 1) * span)
        yield columns, jnp.dot(hidden_ref[...], weight_ref[:, columns], preferred_element_type=F32)


def early_kernel(own_in, other_in, g0_in, u0_in, g1_in, u1_in, g2_in, u2_in, sum_ref, hidden_ref, weight_ref, sems):
    pieces = (g0_in, u0_in, g1_in, u1_in, g2_in, u2_in)
    for columns, total in gather(own_in, other_in, pieces, hidden_ref, weight_ref, sems):
        sum_ref[:, columns] = total


def late_kernel(sum_ref, own_in, other_in, gate_in, up_in, own_ref, theirs_ref, hidden_ref, weight_ref, sems):
    rows = own_in.shape[0]
    for columns, total in gather(own_in, other_in, (gate_in, up_in), hidden_ref, weight_ref, sems):
        total += sum_ref[:, columns]
        own_ref[:, columns] = total[:rows].astype(BF16)
        theirs_ref[:, columns] = total[rows:].astype(BF16)


def join_kernel(own_ref, back_ref, out_ref):
    pack(own_ref[...].astype(F32) + back_ref[...].astype(F32), out_ref, True)


def chosen_of(routes_ref, experts):
    top, tokens = routes_ref.shape
    row = lax.broadcasted_iota(jnp.int32, (experts * SLOTS, tokens), 0)
    number = row // experts
    block = row - number * experts
    planes = experts // ROWS_Y
    named = (block % planes) * ROWS_Y + block // planes
    hits = jnp.zeros(row.shape, F32)
    for k in range(top):
        hits = jnp.where(routes_ref[k : k + 1, :] == named, 1.0, hits)
    before = (
        lax.broadcasted_iota(jnp.int32, (tokens, tokens), 0)
        < lax.broadcasted_iota(jnp.int32, (tokens, tokens), 1)
    ).astype(BF16)
    earlier = jnp.dot(hits.astype(BF16), before, preferred_element_type=F32)
    return named, (hits > 0.5) & (jnp.abs(earlier - number.astype(F32)) < 0.5)


def turn_kernel(routes_ref, hot_ref):
    _, chosen = chosen_of(routes_ref, hot_ref.shape[1] // SLOTS)
    hot_ref[...] = jnp.where(chosen, 1.0, 0.0).T.astype(BF16)


def combine_kernel(hot_ref, back_ref, out_ref):
    tokens, width = out_ref.shape
    experts = back_ref.shape[0]
    slots = hot_ref.shape[1] // experts
    total = jnp.zeros((tokens, width), F32)
    for s in range(slots):
        total += jnp.dot(
            hot_ref[:, s * experts : (s + 1) * experts], unpack(back_ref, s, slots), preferred_element_type=F32
        )
    out_ref[...] = total.astype(BF16)


def body(grad_out, routes, gates, w_gate, w_up, w_down, saved_gate, saved_up):
    experts = lax.axis_size("z") * lax.axis_size("y")
    copies = lax.axis_size("replica")
    tokens, width = grad_out.shape
    slots = saved_gate.shape[3]
    slice_width = w_gate.shape[1]
    rows = experts * slots
    half = width // 2
    chunks = half // 128
    deep = slots * chunks

    def along(a):
        pairs = [(2 * i + k, 2 * ((i + 1 - 2 * k) % LINKS) + k) for i in range(LINKS) for k in range(2)]
        return lax.ppermute(a, "replica", pairs)

    def across(a):
        return lax.ppermute(a, "replica", [(i, i ^ 1) for i in range(copies)])

    def exchange(a):
        return lax.all_to_all(a, ("y", "z"), split_axis=0, concat_axis=0, tiled=True)

    downs, gate_pieces, up_pieces = [w_down[0]], [w_gate[0]], [w_up[0]]
    for _ in range(1, LINKS):
        for pieces in (downs, gate_pieces, up_pieces):
            pieces.append(along(pieces[-1]))

    packed = call(
        place_kernel,
        (routes.T, gates.T, grad_out),
        (jax.ShapeDtypeStruct((experts, 2 * deep, 128), BF16),),
        2 * rows * tokens * width,
        limit=60 << 20,
    )
    arrived = exchange(packed)

    saved = tuple(a[0, 0].transpose(1, 0, 2).reshape(rows, -1) for a in (saved_gate, saved_up))
    hidden_units = LINKS * slice_width
    factor = jax.ShapeDtypeStruct((LINKS, rows, slice_width), F32)
    own_factors = call(factor_kernel, saved, (factor, factor))
    sent = (across(saved[0]), across(saved[1]))
    other_factors = call(factor_kernel, sent, (factor, factor))

    last = 2 * slice_width
    hidden = tuple(jax.ShapeDtypeStruct((rows, n), BF16) for n in (2 * hidden_units - last, last))
    cost = 2 * rows * hidden_units * width
    scratch = (
        pltpu.VMEM((experts // ROWS_Y, ROWS_Y, 2 * deep, 128), BF16),
        pltpu.VMEM((hidden_units, width), BF16),
        pltpu.VMEM((LINKS, rows, slice_width), F32),
        pltpu.VMEM((LINKS, rows, slice_width), F32),
        pltpu.VMEM((rows, width), BF16),
        pltpu.SemaphoreType.DMA((ROWS_Y + 2 * LINKS + 2,)),
    )
    other_rows = across(arrived)

    def hide(packed_rows, factors):
        ins = (packed_rows,) + tuple(downs) + tuple(factors)
        return call(hidden_kernel, ins, hidden, cost, scratch=scratch, spec=AN)

    own_hidden = hide(arrived, own_factors)
    other_hidden = hide(other_rows, other_factors)

    pieces = [piece for both in zip(gate_pieces, up_pieces) for piece in both]

    def room(n):
        return (
            pltpu.VMEM((2 * rows, n), BF16),
            pltpu.VMEM((n, width), BF16),
            pltpu.SemaphoreType.DMA((3, n // slice_width)),
        )

    part = jax.ShapeDtypeStruct((rows, width), BF16)
    early = call(
        early_kernel,
        (own_hidden[0], other_hidden[0]) + tuple(pieces[:-2]),
        (jax.ShapeDtypeStruct((2 * rows, width), F32),),
        3 * cost,
        scratch=room(2 * hidden_units - last),
        spec=AN,
    )
    ours, theirs = call(
        late_kernel,
        (early, own_hidden[1], other_hidden[1]) + tuple(pieces[-2:]),
        (part, part),
        cost,
        scratch=room(last),
        spec=[VM] + [AN] * 4,
    )
    back = across(theirs)
    outgoing = call(join_kernel, (ours, back), (jax.ShapeDtypeStruct((experts, 2 * deep, 128), BF16),))
    returned = exchange(outgoing)
    turned = call(turn_kernel, (routes.T,), (jax.ShapeDtypeStruct((tokens, rows), BF16),))
    return call(combine_kernel, (turned, returned), (jax.ShapeDtypeStruct((tokens, width), BF16),))


def solution(mesh):
    devices = mesh.devices
    split = Mesh(devices.reshape(-1, ROWS_Y, devices.shape[1]), ("z", "y", "replica"))
    in_specs = (
        P(("z", "y", "replica"), None),
        P(("z", "y", "replica"), None),
        P(("z", "y", "replica"), None),
        P(("z", "y"), "replica", None),
        P(("z", "y"), "replica", None),
        P(("z", "y"), "replica", None),
        P(("z", "y"), "replica", None, None, None),
        P(("z", "y"), "replica", None, None, None),
    )
    out_specs = P(("z", "y", "replica"), None)

    return jax.shard_map(body, mesh=split, in_specs=in_specs, out_specs=out_specs, check_vma=False)
```

```python
import jax
import jax.numpy as jnp
from jax import lax
from jax.experimental import pallas as pl
from jax.experimental.pallas import tpu as pltpu
from jax.sharding import Mesh, PartitionSpec as P

F32 = jnp.float32
BF16 = jnp.bfloat16
VM = pl.BlockSpec(memory_space=pltpu.VMEM)
AN = pl.BlockSpec(memory_space=pl.ANY)
LINKS = 4
SLOTS = 3
ROWS_Y = 4


def call(kernel, ins, outs, flops=0, scratch=(), spec=VM, limit=24 << 20):
    moved = sum(a.size * a.dtype.itemsize for a in ins) + sum(o.size * o.dtype.itemsize for o in outs)
    single = len(outs) == 1
    return pl.pallas_call(
        kernel,
        out_shape=outs[0] if single else tuple(outs),
        in_specs=spec if isinstance(spec, list) else [spec] * len(ins),
        out_specs=VM if single else tuple([VM] * len(outs)),
        scratch_shapes=list(scratch),
        compiler_params=pltpu.CompilerParams(vmem_limit_bytes=limit),
        cost_estimate=pl.CostEstimate(flops=flops, bytes_accessed=moved, transcendentals=0),
    )(*ins)


def fetch(copies, sems):
    made = [pltpu.make_async_copy(src, dst, sems.at[n]) for n, (src, dst) in enumerate(copies)]
    for copy in made:
        copy.start()
    return made


def pack(value, out_ref, turned=False):
    experts, deep, lanes = out_ref.shape
    slots = value.shape[0] // experts
    chunks = deep // slots
    span = chunks
    for s in range(slots):
        block = value[s * experts : (s + 1) * experts].astype(BF16)
        stack = jnp.stack([block[:, c * lanes : (c + 1) * lanes] for c in range(span)])
        low = s * chunks
        blocks = jnp.swapaxes(stack, 0, 1)
        if not turned:
            out_ref[:, low : low + span, :] = blocks
            continue
        planes = experts // ROWS_Y
        blocks = blocks.reshape(planes, ROWS_Y, span, lanes)
        for y in range(ROWS_Y):
            out_ref[y * planes : (y + 1) * planes, low : low + span, :] = blocks[:, y]


def unpack(packed_ref, s, slots):
    _, deep, _ = packed_ref.shape
    chunks = deep // slots
    parts = jnp.swapaxes(packed_ref[:, s * chunks : (s + 1) * chunks, :], 0, 1)
    return jnp.concatenate([parts[c] for c in range(chunks)], axis=1)


def place_kernel(routes_ref, gates_ref, grad_ref, out_ref):
    named, chosen = chosen_of(routes_ref, out_ref.shape[0])
    weight = jnp.zeros(named.shape, F32)
    for k in range(routes_ref.shape[0]):
        weight = jnp.where(routes_ref[k : k + 1, :] == named, gates_ref[k : k + 1, :], weight)
    weight = jnp.sum(jnp.where(chosen, weight, 0.0), axis=1, keepdims=True)
    hot = jnp.where(chosen, 1.0, 0.0).astype(BF16)
    pack(weight * jnp.dot(hot, grad_ref[...], preferred_element_type=F32), out_ref)


def factor_kernel(gate_ref, up_ref, gf_ref, uf_ref):
    slice_width = gf_ref.shape[2]
    replica = lax.axis_index("replica")
    link, turn = replica >> 1, 2 * (replica & 1) - 1
    first = turn < 0
    for q in range(LINKS):
        low = 2 * q * slice_width
        mid, high = low + slice_width, low + 2 * slice_width
        g = jnp.where(first, gate_ref[:, low:mid].astype(F32), gate_ref[:, mid:high].astype(F32))
        u = jnp.where(first, up_ref[:, low:mid].astype(F32), up_ref[:, mid:high].astype(F32))
        sig = jax.nn.sigmoid(g)
        step = ((q - link) * turn + 2 * LINKS) & (LINKS - 1)
        uf_ref[step] = g * sig
        gf_ref[step] = u * sig * (1.0 + g * (1.0 - sig))


def hidden_kernel(
    packed_in, down0_in, down1_in, down2_in, down3_in, gf_in, uf_in,
    early_ref, late_ref, packed_ref, down_ref, gf_ref, uf_ref, rows_ref, sems,
):
    planes, across_y, deep, lanes = packed_ref.shape
    copies = [(packed_in.at[pl.ds(y * planes, planes)], packed_ref.at[:, y]) for y in range(across_y)]
    half = down_ref.shape[1] // 2
    width = down0_in.shape[0]
    downs = (down0_in, down1_in, down2_in, down3_in)
    for n in range(2):
        columns = pl.ds(n * half, half)
        for step, piece in enumerate(downs):
            place = pl.ds(step * width, width)
            copies.append((piece.at[:, columns], down_ref.at[place, columns]))
    copies = fetch(copies + [(gf_in, gf_ref), (uf_in, uf_ref)], sems)
    for copy in copies[:across_y]:
        copy.wait()
    experts = planes * across_y
    slots = rows_ref.shape[0] // experts
    packed = packed_ref[...].reshape(experts, deep, lanes)
    for s in range(slots):
        rows_ref[s * experts : (s + 1) * experts, :] = unpack(packed, s, slots)
    grad = jnp.zeros((rows_ref.shape[0], down_ref.shape[0]), F32)
    for n in range(2):
        for copy in copies[across_y + n * LINKS : across_y + (n + 1) * LINKS]:
            copy.wait()
        columns = slice(n * half, (n + 1) * half)
        grad += lax.dot_general(
            rows_ref[:, columns], down_ref[:, columns], (((1,), (1,)), ((), ())), preferred_element_type=F32
        )
    for copy in copies[across_y + 2 * LINKS :]:
        copy.wait()
    for step in range(LINKS):
        part = grad[:, step * width : (step + 1) * width]
        out_ref, low = (early_ref, 2 * step * width) if step < LINKS - 1 else (late_ref, 0)
        out_ref[:, low : low + width] = (part * gf_ref[step]).astype(BF16)
        out_ref[:, low + width : low + 2 * width] = (part * uf_ref[step]).astype(BF16)


def gather(own_in, other_in, pieces, hidden_ref, weight_ref, sems):
    rows, width = own_in.shape[0], pieces[0].shape[0]
    parts = sems.shape[0] - 1
    span = weight_ref.shape[1] // parts
    begun = fetch(
        [(own_in, hidden_ref.at[pl.ds(0, rows), :]), (other_in, hidden_ref.at[pl.ds(rows, rows), :])], sems.at[0]
    )
    blocks = []
    for n in range(parts):
        columns = pl.ds(n * span, span)
        copies = [
            (piece.at[:, columns], weight_ref.at[pl.ds(k * width, width), columns]) for k, piece in enumerate(pieces)
        ]
        blocks.append(fetch(copies, sems.at[n + 1]))
    for copy in begun:
        copy.wait()
    for n in range(parts):
        for copy in blocks[n]:
            copy.wait()
        columns = slice(n * span, (n + 1) * span)
        yield columns, jnp.dot(hidden_ref[...], weight_ref[:, columns], preferred_element_type=F32)


def early_kernel(own_in, other_in, g0_in, u0_in, g1_in, u1_in, g2_in, u2_in, sum_ref, hidden_ref, weight_ref, sems):
    pieces = (g0_in, u0_in, g1_in, u1_in, g2_in, u2_in)
    for columns, total in gather(own_in, other_in, pieces, hidden_ref, weight_ref, sems):
        sum_ref[:, columns] = total


def late_kernel(sum_ref, own_in, other_in, gate_in, up_in, own_ref, theirs_ref, hidden_ref, weight_ref, sems):
    rows = own_in.shape[0]
    for columns, total in gather(own_in, other_in, (gate_in, up_in), hidden_ref, weight_ref, sems):
        total += sum_ref[:, columns]
        own_ref[:, columns] = total[:rows].astype(BF16)
        theirs_ref[:, columns] = total[rows:].astype(BF16)


def join_kernel(own_ref, back_ref, out_ref):
    pack(own_ref[...].astype(F32) + back_ref[...].astype(F32), out_ref, True)


def chosen_of(routes_ref, experts):
    top, tokens = routes_ref.shape
    row = lax.broadcasted_iota(jnp.int32, (experts * SLOTS, tokens), 0)
    number = row // experts
    block = row - number * experts
    planes = experts // ROWS_Y
    named = (block % planes) * ROWS_Y + block // planes
    hits = jnp.zeros(row.shape, F32)
    for k in range(top):
        hits = jnp.where(routes_ref[k : k + 1, :] == named, 1.0, hits)
    before = (
        lax.broadcasted_iota(jnp.int32, (tokens, tokens), 0)
        < lax.broadcasted_iota(jnp.int32, (tokens, tokens), 1)
    ).astype(BF16)
    earlier = jnp.dot(hits.astype(BF16), before, preferred_element_type=F32)
    return named, (hits > 0.5) & (jnp.abs(earlier - number.astype(F32)) < 0.5)


def turn_kernel(routes_ref, hot_ref):
    _, chosen = chosen_of(routes_ref, hot_ref.shape[1] // SLOTS)
    hot_ref[...] = jnp.where(chosen, 1.0, 0.0).T.astype(BF16)


def combine_kernel(hot_ref, back_ref, out_ref):
    tokens, width = out_ref.shape
    experts = back_ref.shape[0]
    slots = hot_ref.shape[1] // experts
    total = jnp.zeros((tokens, width), F32)
    for s in range(slots):
        total += jnp.dot(
            hot_ref[:, s * experts : (s + 1) * experts], unpack(back_ref, s, slots), preferred_element_type=F32
        )
    out_ref[...] = total.astype(BF16)


def body(grad_out, routes, gates, w_gate, w_up, w_down, saved_gate, saved_up):
    experts = lax.axis_size("z") * lax.axis_size("y")
    copies = lax.axis_size("replica")
    tokens, width = grad_out.shape
    slots = saved_gate.shape[3]
    slice_width = w_gate.shape[1]
    rows = experts * slots
    half = width // 2
    chunks = half // 128
    deep = slots * chunks

    def along(a):
        pairs = [(2 * i + k, 2 * ((i + 1 - 2 * k) % LINKS) + k) for i in range(LINKS) for k in range(2)]
        return lax.ppermute(a, "replica", pairs)

    def across(a):
        return lax.ppermute(a, "replica", [(i, i ^ 1) for i in range(copies)])

    def exchange(a):
        return lax.all_to_all(a, ("y", "z"), split_axis=0, concat_axis=0, tiled=True)

    downs, gate_pieces, up_pieces = [w_down[0]], [w_gate[0]], [w_up[0]]
    for _ in range(1, LINKS):
        for pieces in (downs, gate_pieces, up_pieces):
            pieces.append(along(pieces[-1]))

    packed = call(
        place_kernel,
        (routes.T, gates.T, grad_out),
        (jax.ShapeDtypeStruct((experts, 2 * deep, 128), BF16),),
        2 * rows * tokens * width,
        limit=60 << 20,
    )
    arrived = exchange(packed)

    saved = tuple(a[0, 0].transpose(1, 0, 2).reshape(rows, -1) for a in (saved_gate, saved_up))
    hidden_units = LINKS * slice_width
    factor = jax.ShapeDtypeStruct((LINKS, rows, slice_width), F32)
    own_factors = call(factor_kernel, saved, (factor, factor))
    sent = (across(saved[0]), across(saved[1]))
    other_factors = call(factor_kernel, sent, (factor, factor))

    last = 2 * slice_width
    hidden = tuple(jax.ShapeDtypeStruct((rows, n), BF16) for n in (2 * hidden_units - last, last))
    cost = 2 * rows * hidden_units * width
    scratch = (
        pltpu.VMEM((experts // ROWS_Y, ROWS_Y, 2 * deep, 128), BF16),
        pltpu.VMEM((hidden_units, width), BF16),
        pltpu.VMEM((LINKS, rows, slice_width), F32),
        pltpu.VMEM((LINKS, rows, slice_width), F32),
        pltpu.VMEM((rows, width), BF16),
        pltpu.SemaphoreType.DMA((ROWS_Y + 2 * LINKS + 2,)),
    )
    other_rows = across(arrived)

    def hide(packed_rows, factors, limit):
        ins = (packed_rows,) + tuple(downs) + tuple(factors)
        return call(hidden_kernel, ins, hidden, cost, scratch=scratch, spec=AN, limit=limit)

    own_hidden = hide(arrived, own_factors, 50 << 20)
    other_hidden = hide(other_rows, other_factors, 50 << 20)

    pieces = [piece for both in zip(gate_pieces, up_pieces) for piece in both]

    def room(n):
        return (
            pltpu.VMEM((2 * rows, n), BF16),
            pltpu.VMEM((n, width), BF16),
            pltpu.SemaphoreType.DMA((3, n // slice_width)),
        )

    part = jax.ShapeDtypeStruct((rows, width), BF16)
    early = call(
        early_kernel,
        (own_hidden[0], other_hidden[0]) + tuple(pieces[:-2]),
        (jax.ShapeDtypeStruct((2 * rows, width), F32),),
        3 * cost,
        scratch=room(2 * hidden_units - last),
        spec=AN,
    )
    ours, theirs = call(
        late_kernel,
        (early, own_hidden[1], other_hidden[1]) + tuple(pieces[-2:]),
        (part, part),
        cost,
        scratch=room(last),
        spec=[VM] + [AN] * 4,
    )
    back = across(theirs)
    outgoing = call(join_kernel, (ours, back), (jax.ShapeDtypeStruct((experts, 2 * deep, 128), BF16),))
    returned = exchange(outgoing)
    turned = call(turn_kernel, (routes.T,), (jax.ShapeDtypeStruct((tokens, rows), BF16),))
    return call(combine_kernel, (turned, returned), (jax.ShapeDtypeStruct((tokens, width), BF16),))


def solution(mesh):
    devices = mesh.devices
    split = Mesh(devices.reshape(-1, ROWS_Y, devices.shape[1]), ("z", "y", "replica"))
    in_specs = (
        P(("z", "y", "replica"), None),
        P(("z", "y", "replica"), None),
        P(("z", "y", "replica"), None),
        P(("z", "y"), "replica", None),
        P(("z", "y"), "replica", None),
        P(("z", "y"), "replica", None),
        P(("z", "y"), "replica", None, None, None),
        P(("z", "y"), "replica", None, None, None),
    )
    out_specs = P(("z", "y", "replica"), None)

    return jax.shard_map(body, mesh=split, in_specs=in_specs, out_specs=out_specs, check_vma=False)
```

```python
import jax
import jax.numpy as jnp
from jax import lax
from jax.experimental import pallas as pl
from jax.experimental.pallas import tpu as pltpu
from jax.sharding import Mesh, PartitionSpec as P

F32 = jnp.float32
BF16 = jnp.bfloat16
VM = pl.BlockSpec(memory_space=pltpu.VMEM)
AN = pl.BlockSpec(memory_space=pl.ANY)
LINKS = 4
SLOTS = 3
ROWS_Y = 4


def call(kernel, ins, outs, flops=0, scratch=(), spec=VM, limit=24 << 20):
    moved = sum(a.size * a.dtype.itemsize for a in ins) + sum(o.size * o.dtype.itemsize for o in outs)
    single = len(outs) == 1
    return pl.pallas_call(
        kernel,
        out_shape=outs[0] if single else tuple(outs),
        in_specs=spec if isinstance(spec, list) else [spec] * len(ins),
        out_specs=VM if single else tuple([VM] * len(outs)),
        scratch_shapes=list(scratch),
        compiler_params=pltpu.CompilerParams(vmem_limit_bytes=limit),
        cost_estimate=pl.CostEstimate(flops=flops, bytes_accessed=moved, transcendentals=0),
    )(*ins)


def fetch(copies, sems):
    made = [pltpu.make_async_copy(src, dst, sems.at[n]) for n, (src, dst) in enumerate(copies)]
    for copy in made:
        copy.start()
    return made


def pack(value, out_ref, turned=False):
    experts, deep, lanes = out_ref.shape
    slots = value.shape[0] // experts
    chunks = deep // slots
    span = chunks
    for s in range(slots):
        block = value[s * experts : (s + 1) * experts].astype(BF16)
        stack = jnp.stack([block[:, c * lanes : (c + 1) * lanes] for c in range(span)])
        low = s * chunks
        blocks = jnp.swapaxes(stack, 0, 1)
        if not turned:
            out_ref[:, low : low + span, :] = blocks
            continue
        planes = experts // ROWS_Y
        blocks = blocks.reshape(planes, ROWS_Y, span, lanes)
        for y in range(ROWS_Y):
            out_ref[y * planes : (y + 1) * planes, low : low + span, :] = blocks[:, y]


def unpack(packed_ref, s, slots):
    _, deep, _ = packed_ref.shape
    chunks = deep // slots
    parts = jnp.swapaxes(packed_ref[:, s * chunks : (s + 1) * chunks, :], 0, 1)
    return jnp.concatenate([parts[c] for c in range(chunks)], axis=1)


def place_kernel(routes_ref, gates_ref, grad_ref, out_ref):
    named, chosen = chosen_of(routes_ref, out_ref.shape[0])
    weight = jnp.zeros(named.shape, F32)
    for k in range(routes_ref.shape[0]):
        weight = jnp.where(routes_ref[k : k + 1, :] == named, gates_ref[k : k + 1, :], weight)
    weight = jnp.sum(jnp.where(chosen, weight, 0.0), axis=1, keepdims=True)
    hot = jnp.where(chosen, 1.0, 0.0).astype(BF16)
    pack(weight * jnp.dot(hot, grad_ref[...], preferred_element_type=F32), out_ref)


def factor_kernel(gate_ref, up_ref, gf_ref, uf_ref):
    slice_width = gf_ref.shape[1] // LINKS
    replica = lax.axis_index("replica")
    link, turn = replica >> 1, 2 * (replica & 1) - 1
    first = turn < 0
    gates, ups = [], []
    for q in range(LINKS):
        low = 2 * q * slice_width
        mid, high = low + slice_width, low + 2 * slice_width
        g = jnp.where(first, gate_ref[:, low:mid].astype(F32), gate_ref[:, mid:high].astype(F32))
        u = jnp.where(first, up_ref[:, low:mid].astype(F32), up_ref[:, mid:high].astype(F32))
        sig = jax.nn.sigmoid(g)
        ups.append(g * sig)
        gates.append(u * sig * (1.0 + g * (1.0 - sig)))
    for step in range(LINKS):
        held = (link + step * turn + LINKS) & (LINKS - 1)
        place = slice(step * slice_width, (step + 1) * slice_width)
        for values, ref in ((gates, gf_ref), (ups, uf_ref)):
            value = values[0]
            for q in range(1, LINKS):
                value = jnp.where(held == q, values[q], value)
            ref[:, place] = value


def hidden_kernel(
    packed_in, down0_in, down1_in, down2_in, down3_in, gf_in, uf_in,
    early_ref, late_ref, packed_ref, down_ref, gf_ref, uf_ref, rows_ref, sems,
):
    planes, across_y, deep, lanes = packed_ref.shape
    copies = [(packed_in.at[pl.ds(y * planes, planes)], packed_ref.at[:, y]) for y in range(across_y)]
    half = down_ref.shape[1] // 2
    width = down0_in.shape[0]
    downs = (down0_in, down1_in, down2_in, down3_in)
    for n in range(2):
        columns = pl.ds(n * half, half)
        for step, piece in enumerate(downs):
            place = pl.ds(step * width, width)
            copies.append((piece.at[:, columns], down_ref.at[place, columns]))
    copies = fetch(copies + [(gf_in, gf_ref), (uf_in, uf_ref)], sems)
    for copy in copies[:across_y]:
        copy.wait()
    experts = planes * across_y
    slots = rows_ref.shape[0] // experts
    packed = packed_ref[...].reshape(experts, deep, lanes)
    for s in range(slots):
        rows_ref[s * experts : (s + 1) * experts, :] = unpack(packed, s, slots)
    grad = jnp.zeros((rows_ref.shape[0], down_ref.shape[0]), F32)
    for n in range(2):
        for copy in copies[across_y + n * LINKS : across_y + (n + 1) * LINKS]:
            copy.wait()
        columns = slice(n * half, (n + 1) * half)
        grad += lax.dot_general(
            rows_ref[:, columns], down_ref[:, columns], (((1,), (1,)), ((), ())), preferred_element_type=F32
        )
    for copy in copies[across_y + 2 * LINKS :]:
        copy.wait()
    cut = (LINKS - 1) * width
    for factor_ref, half in ((gf_ref, 0), (uf_ref, 1)):
        value = (grad * factor_ref[...]).astype(BF16)
        early_ref[:, half * cut : (half + 1) * cut] = value[:, :cut]
        late_ref[:, half * width : (half + 1) * width] = value[:, cut:]


def gather(own_in, other_in, pieces, hidden_ref, weight_ref, sems):
    rows, width = own_in.shape[0], pieces[0].shape[0]
    parts = sems.shape[0] - 1
    span = weight_ref.shape[1] // parts
    begun = fetch(
        [(own_in, hidden_ref.at[pl.ds(0, rows), :]), (other_in, hidden_ref.at[pl.ds(rows, rows), :])], sems.at[0]
    )
    blocks = []
    for n in range(parts):
        columns = pl.ds(n * span, span)
        copies = [
            (piece.at[:, columns], weight_ref.at[pl.ds(k * width, width), columns]) for k, piece in enumerate(pieces)
        ]
        blocks.append(fetch(copies, sems.at[n + 1]))
    for copy in begun:
        copy.wait()
    for n in range(parts):
        for copy in blocks[n]:
            copy.wait()
        columns = slice(n * span, (n + 1) * span)
        yield columns, jnp.dot(hidden_ref[...], weight_ref[:, columns], preferred_element_type=F32)


def early_kernel(own_in, other_in, g0_in, g1_in, g2_in, u0_in, u1_in, u2_in, sum_ref, hidden_ref, weight_ref, sems):
    pieces = (g0_in, g1_in, g2_in, u0_in, u1_in, u2_in)
    for columns, total in gather(own_in, other_in, pieces, hidden_ref, weight_ref, sems):
        sum_ref[:, columns] = total


def late_kernel(sum_ref, own_in, other_in, gate_in, up_in, own_ref, theirs_ref, hidden_ref, weight_ref, sems):
    rows = own_in.shape[0]
    for columns, total in gather(own_in, other_in, (gate_in, up_in), hidden_ref, weight_ref, sems):
        total += sum_ref[:, columns]
        own_ref[:, columns] = total[:rows].astype(BF16)
        theirs_ref[:, columns] = total[rows:].astype(BF16)


def join_kernel(own_ref, back_ref, out_ref):
    pack(own_ref[...].astype(F32) + back_ref[...].astype(F32), out_ref, True)


def chosen_of(routes_ref, experts):
    top, tokens = routes_ref.shape
    row = lax.broadcasted_iota(jnp.int32, (experts * SLOTS, tokens), 0)
    number = row // experts
    block = row - number * experts
    planes = experts // ROWS_Y
    named = (block % planes) * ROWS_Y + block // planes
    hits = jnp.zeros(row.shape, F32)
    for k in range(top):
        hits = jnp.where(routes_ref[k : k + 1, :] == named, 1.0, hits)
    before = (
        lax.broadcasted_iota(jnp.int32, (tokens, tokens), 0)
        < lax.broadcasted_iota(jnp.int32, (tokens, tokens), 1)
    ).astype(BF16)
    earlier = jnp.dot(hits.astype(BF16), before, preferred_element_type=F32)
    return named, (hits > 0.5) & (jnp.abs(earlier - number.astype(F32)) < 0.5)


def turn_kernel(routes_ref, hot_ref):
    _, chosen = chosen_of(routes_ref, hot_ref.shape[1] // SLOTS)
    hot_ref[...] = jnp.where(chosen, 1.0, 0.0).T.astype(BF16)


def combine_kernel(hot_ref, back_ref, out_ref):
    tokens, width = out_ref.shape
    experts = back_ref.shape[0]
    slots = hot_ref.shape[1] // experts
    total = jnp.zeros((tokens, width), F32)
    for s in range(slots):
        total += jnp.dot(
            hot_ref[:, s * experts : (s + 1) * experts], unpack(back_ref, s, slots), preferred_element_type=F32
        )
    out_ref[...] = total.astype(BF16)


def body(grad_out, routes, gates, w_gate, w_up, w_down, saved_gate, saved_up):
    experts = lax.axis_size("z") * lax.axis_size("y")
    copies = lax.axis_size("replica")
    tokens, width = grad_out.shape
    slots = saved_gate.shape[3]
    slice_width = w_gate.shape[1]
    rows = experts * slots
    half = width // 2
    chunks = half // 128
    deep = slots * chunks

    def along(a):
        pairs = [(2 * i + k, 2 * ((i + 1 - 2 * k) % LINKS) + k) for i in range(LINKS) for k in range(2)]
        return lax.ppermute(a, "replica", pairs)

    def across(a):
        return lax.ppermute(a, "replica", [(i, i ^ 1) for i in range(copies)])

    def exchange(a):
        return lax.all_to_all(a, ("y", "z"), split_axis=0, concat_axis=0, tiled=True)

    downs, gate_pieces, up_pieces = [w_down[0]], [w_gate[0]], [w_up[0]]
    for _ in range(1, LINKS):
        for pieces in (downs, gate_pieces, up_pieces):
            pieces.append(along(pieces[-1]))

    packed = call(
        place_kernel,
        (routes.T, gates.T, grad_out),
        (jax.ShapeDtypeStruct((experts, 2 * deep, 128), BF16),),
        2 * rows * tokens * width,
        limit=60 << 20,
    )
    arrived = exchange(packed)

    saved = tuple(a[0, 0].transpose(1, 0, 2).reshape(rows, -1) for a in (saved_gate, saved_up))
    hidden_units = LINKS * slice_width
    factor = jax.ShapeDtypeStruct((rows, hidden_units), F32)
    own_factors = call(factor_kernel, saved, (factor, factor))
    sent = (across(saved[0]), across(saved[1]))
    other_factors = call(factor_kernel, sent, (factor, factor))

    last = 2 * slice_width
    hidden = tuple(jax.ShapeDtypeStruct((rows, n), BF16) for n in (2 * hidden_units - last, last))
    cost = 2 * rows * hidden_units * width
    scratch = (
        pltpu.VMEM((experts // ROWS_Y, ROWS_Y, 2 * deep, 128), BF16),
        pltpu.VMEM((hidden_units, width), BF16),
        pltpu.VMEM((rows, hidden_units), F32),
        pltpu.VMEM((rows, hidden_units), F32),
        pltpu.VMEM((rows, width), BF16),
        pltpu.SemaphoreType.DMA((ROWS_Y + 2 * LINKS + 2,)),
    )
    other_rows = across(arrived)

    def hide(packed_rows, factors, limit):
        ins = (packed_rows,) + tuple(downs) + tuple(factors)
        return call(hidden_kernel, ins, hidden, cost, scratch=scratch, spec=AN, limit=limit)

    own_hidden = hide(arrived, own_factors, 53 << 20)
    other_hidden = hide(other_rows, other_factors, 53 << 20)


    def room(n):
        return (
            pltpu.VMEM((2 * rows, n), BF16),
            pltpu.VMEM((n, width), BF16),
            pltpu.SemaphoreType.DMA((3, n // slice_width)),
        )

    part = jax.ShapeDtypeStruct((rows, width), BF16)
    early = call(
        early_kernel,
        (own_hidden[0], other_hidden[0]) + tuple(gate_pieces[:-1] + up_pieces[:-1]),
        (jax.ShapeDtypeStruct((2 * rows, width), F32),),
        3 * cost,
        scratch=room(2 * hidden_units - last),
        spec=AN,
    )
    ours, theirs = call(
        late_kernel,
        (early, own_hidden[1], other_hidden[1]) + (gate_pieces[-1], up_pieces[-1]),
        (part, part),
        cost,
        scratch=room(last),
        spec=[VM] + [AN] * 4,
    )
    back = across(theirs)
    outgoing = call(join_kernel, (ours, back), (jax.ShapeDtypeStruct((experts, 2 * deep, 128), BF16),))
    returned = exchange(outgoing)
    turned = call(turn_kernel, (routes.T,), (jax.ShapeDtypeStruct((tokens, rows), BF16),))
    return call(combine_kernel, (turned, returned), (jax.ShapeDtypeStruct((tokens, width), BF16),))


def solution(mesh):
    devices = mesh.devices
    split = Mesh(devices.reshape(-1, ROWS_Y, devices.shape[1]), ("z", "y", "replica"))
    in_specs = (
        P(("z", "y", "replica"), None),
        P(("z", "y", "replica"), None),
        P(("z", "y", "replica"), None),
        P(("z", "y"), "replica", None),
        P(("z", "y"), "replica", None),
        P(("z", "y"), "replica", None),
        P(("z", "y"), "replica", None, None, None),
        P(("z", "y"), "replica", None, None, None),
    )
    out_specs = P(("z", "y", "replica"), None)

    return jax.shard_map(body, mesh=split, in_specs=in_specs, out_specs=out_specs, check_vma=False)
```
